256 devices in a mesh: dp: 64 (over x, z_hi, y), tensor: 4 (over z_lo, core).
Axes of the slice: x: 4, y: 4, z: 8 (z_hi: 4, z_lo: 2; z = z_hi * 2 + z_lo), core: 2. Of those that a mesh axis runs over, the one named last changes fastest.
Arguments:
- tokens: bfloat16 [49152, 2048], P('dp'), may hold values from -6 to 6
- targets: bfloat16 [49152, 2048], P('dp'), may hold values from -6 to 6
- up_weight: bfloat16 [64, 64, 256, 256], P('dp', 'tensor'), may hold values from -6 to 6
- down_weight: bfloat16 [64, 64, 256, 256], P('dp', 'tensor'), may hold values from -6 to 6
- block_rows: int32 [64], P('tensor'), may hold values from 0 to 7, as said below
- block_columns: int32 [64], P('tensor'), may hold values from 0 to 7, as said below
Outputs:
- new_up: bfloat16 [64, 64, 256, 256], P('dp', 'tensor')
- new_down: bfloat16 [64, 64, 256, 256], P('dp', 'tensor')
- input_grad: bfloat16 [49152, 2048], P('dp', 'tensor')
The draws below stay inside these ranges and needn't reach their ends.
Inputs may be any that keep to these rules, and one draw needn't show every extreme that they name: Within each tensor shard the 16 blocks sit at distinct (block_rows, block_columns) positions, and every hidden block of a shard holds exactly 2 of them; up_weight and down_weight share this pattern. `block_columns`: hidden block indices within a shard.
All inputs are finite; a program needn't handle non-finite values.
Results may differ from the reference program's by a relative error of at most 0.015.
Values may be sent and summed in bfloat16 or wider, within the bound.
A program may use at most 128 MiB of HBM per device.

```python
import jax
import jax.numpy as jnp
from jax import lax

D = 2048
H = 8192
BLK = 256
TOK = 768
BLOCKS = 16
N_DP = 64
N_TENSOR = 4


def pattern_pair(key):
    model_blocks = D // BLK
    shard_hidden = H // (N_TENSOR * BLK)
    per_column = model_blocks // 4

    def one_shard(shard_key):
        row_perm = jax.random.permutation(jax.random.fold_in(shard_key, 1), model_blocks)
        col_shift = jax.random.permutation(jax.random.fold_in(shard_key, 2), shard_hidden)
        order = jax.random.permutation(jax.random.fold_in(shard_key, 3), shard_hidden * per_column)
        col_ids = jnp.repeat(jnp.arange(shard_hidden), per_column)
        offsets = jnp.tile(jnp.arange(per_column), shard_hidden) * 4
        rows = row_perm[(col_shift[col_ids] + offsets) % model_blocks]
        return (rows[order].astype(jnp.int32), col_ids[order].astype(jnp.int32))
    keys = jax.random.split(jax.random.fold_in(key, 11), N_TENSOR)
    rows, cols = jax.vmap(one_shard)(keys)
    return (rows.reshape(-1), cols.reshape(-1))


def draw_block_rows(key, part):
    return pattern_pair(key)[0]


def draw_block_columns(key, part):
    return pattern_pair(key)[1]


def levels(stream_key, extent, cuts, low, largest):
    gain = 1.0
    for position, blocks in cuts:
        steps = jax.random.uniform(jax.random.fold_in(jax.random.fold_in(stream_key, 6), position), (blocks,), jnp.float32, low / len(cuts), largest / len(cuts))
        gain = gain * jnp.repeat(jnp.exp(steps), extent[position] // blocks).reshape((-1,) + (1,) * (len(extent) - 1 - position))
    return gain


def bell_draw(own_key, shape, spread, most, shards=(), held_as=jnp.bfloat16):
    entries = spread * jax.random.normal(own_key, shape, jnp.float32)
    if shards:
        entries = entries * levels(own_key, shape, shards, -0.22, 0.18)
    return jnp.clip(entries, -most, most).astype(held_as)


def setup_inputs(seed: int = 0) -> dict:
    streams_of = jax.random.split(jax.random.key(seed), 7)
    tokens = bell_draw(streams_of[0], (N_DP * TOK, D), 1.0, 6.0, ((0, 64),))
    targets = bell_draw(streams_of[1], (N_DP * TOK, D), 1.0, 6.0, ((0, 64),))
    up_weight = bell_draw(streams_of[2], (N_DP, N_TENSOR * BLOCKS, BLK, BLK), 1.0, 6.0, ((0, 64), (1, 4)))
    down_weight = bell_draw(streams_of[3], (N_DP, N_TENSOR * BLOCKS, BLK, BLK), 1.0, 6.0, ((0, 64), (1, 4)))
    block_rows = draw_block_rows(jax.random.fold_in(streams_of[6], 71), 0)
    block_columns = draw_block_columns(jax.random.fold_in(streams_of[6], 71), 0)
    return dict(tokens=tokens, targets=targets, up_weight=up_weight, down_weight=down_weight, block_rows=block_rows, block_columns=block_columns)


step_rate = 0.5


def replica_step(tok_rows, target_rows, up_mine, down_mine, up_peer, down_peer, block_rows, block_columns):
    model_blocks = D // BLK
    shard_hidden = H // (N_TENSOR * BLK)
    hidden_blocks = shard_hidden * N_TENSOR
    total_blocks = N_TENSOR * BLOCKS
    scale_in = (D // 4) ** -0.5
    scale_out = (H // 4) ** -0.5
    shard_of = (jnp.arange(total_blocks) // BLOCKS).astype(jnp.int32)
    global_cols = (shard_of * shard_hidden + block_columns).astype(jnp.int32)
    row_ids = (shard_of * model_blocks + block_rows).astype(jnp.int32)
    up_float = up_mine.astype(jnp.float32)
    down_float = down_mine.astype(jnp.float32)
    tok_blocks = jnp.transpose(tok_rows.reshape(TOK, model_blocks, BLK)[:, block_rows, :], (1, 0, 2)).astype(jnp.float32)
    first = jnp.einsum("ntk,nkj->ntj", tok_blocks, up_float)
    hidden_pre = jax.ops.segment_sum(first, global_cols, num_segments=hidden_blocks) * scale_in
    active = jax.nn.silu(hidden_pre).astype(jnp.bfloat16)
    active_blocks = active[global_cols].astype(jnp.float32)
    second = jnp.einsum("ntj,njk->ntk", active_blocks, down_float)
    out_parts = (jax.ops.segment_sum(second, row_ids, num_segments=N_TENSOR * model_blocks) * scale_out).astype(jnp.bfloat16)
    out_parts = lax.optimization_barrier(out_parts)
    out_sum = out_parts.astype(jnp.float32).reshape(N_TENSOR, model_blocks, TOK, BLK).sum(0)
    output = jnp.transpose(out_sum, (1, 0, 2)).reshape(TOK, D)
    error = (output - target_rows.astype(jnp.float32)).astype(jnp.bfloat16)
    error_blocks = jnp.transpose(error.reshape(TOK, model_blocks, BLK)[:, block_rows, :], (1, 0, 2)).astype(jnp.float32)
    grad_down = scale_out * jnp.einsum("ntj,ntk->njk", active_blocks, error_blocks)
    dact_blocks = jnp.einsum("ntk,njk->ntj", error_blocks, down_float)
    dact = jax.ops.segment_sum(dact_blocks, global_cols, num_segments=hidden_blocks) * scale_out
    sigma = jax.nn.sigmoid(hidden_pre)
    dpre = (dact * sigma * (1.0 + hidden_pre * (1.0 - sigma))).astype(jnp.bfloat16)
    dpre_blocks = dpre[global_cols].astype(jnp.float32)
    grad_up = scale_in * jnp.einsum("ntk,ntj->nkj", tok_blocks, dpre_blocks)
    back_blocks = jnp.einsum("ntj,nkj->ntk", dpre_blocks, up_float)
    back_parts = (jax.ops.segment_sum(back_blocks, row_ids, num_segments=N_TENSOR * model_blocks) * scale_in).astype(jnp.bfloat16)
    back_parts = lax.optimization_barrier(back_parts)
    back_sum = back_parts.astype(jnp.float32).reshape(N_TENSOR, model_blocks, TOK, BLK).sum(0)
    input_grad = jnp.transpose(back_sum, (1, 0, 2)).reshape(TOK, D).astype(jnp.bfloat16)
    new_up = (0.5 * (up_float + up_peer.astype(jnp.float32)) - step_rate * grad_up).astype(jnp.bfloat16)
    new_down = (0.5 * (down_float + down_peer.astype(jnp.float32)) - step_rate * grad_down).astype(jnp.bfloat16)
    return new_up, new_down, input_grad


def reference(tokens, targets, up_weight, down_weight, block_rows, block_columns):
    level = (N_DP.bit_length() - 1) // 2
    tok_all = tokens.reshape(N_DP, TOK, D)
    target_all = targets.reshape(N_DP, TOK, D)

    def one_replica(replica):
        partner = jnp.bitwise_xor(replica, jnp.int32(1 << level)).astype(jnp.int32)
        return replica_step(tok_all[replica], target_all[replica], up_weight[replica], down_weight[replica],
                            up_weight[partner], down_weight[partner], block_rows, block_columns)

    new_up, new_down, input_grad = lax.map(one_replica, jnp.arange(N_DP, dtype=jnp.int32))
    return new_up, new_down, input_grad.reshape(N_DP * TOK, D)
```

```python
import jax
import jax.numpy as jnp
from jax import lax
from jax.experimental import pallas as pl
from jax.experimental.pallas import tpu as pltpu
from jax.sharding import PartitionSpec as P


D = 2048
H = 8192
STEP_RATE = 0.5
MESH = pl.DeviceIdType.MESH
F32 = jnp.float32
BF16 = jnp.bfloat16


def order_blocks(columns_ref, count_ref, place_ref):
    for h in range(count_ref.shape[0]):
        count_ref[h] = 0
    for k in range(columns_ref.shape[0]):
        h = columns_ref[k]
        seen = count_ref[h]
        place_ref[2 * h + seen] = k
        count_ref[h] = seen + 1


def sigmoid(v):
    return 1.0 / (1.0 + jnp.exp(-v))


def dot(a, b, contract):
    return lax.dot_general(a, b, (contract, ((), ())), preferred_element_type=F32)


NN = ((1,), (0,))
NT = ((1,), (1,))
TN = ((0,), (0,))


def forward_kernel(
    scale_in, scale_out, tile, rows_ref, columns_ref, tok_ref, up_ref, down_ref,
    pre_ref, part_ref, acc_ref, count_ref, place_ref,
):
    hidden, tok_count, block = pre_ref.shape
    model = acc_ref.shape[0]
    order_blocks(columns_ref, count_ref, place_ref)

    @pl.loop(0, tok_count // tile)
    def _(i):
        span = pl.ds(pl.multiple_of(i * tile, tile), tile)
        acc_ref[...] = jnp.zeros_like(acc_ref)

        @pl.loop(0, hidden)
        def _(h):
            ka, kb = place_ref[2 * h], place_ref[2 * h + 1]
            ra, rb = rows_ref[ka], rows_ref[kb]
            xa = tok_ref[span, pl.ds(pl.multiple_of(ra * block, block), block)]
            xb = tok_ref[span, pl.ds(pl.multiple_of(rb * block, block), block)]
            pre = (dot(xa, up_ref[ka], NN) + dot(xb, up_ref[kb], NN)) * scale_in
            pre_ref[h, span, :] = pre
            act = (pre * sigmoid(pre)).astype(BF16)
            acc_ref[ra] += dot(act, down_ref[ka], NN)
            acc_ref[rb] += dot(act, down_ref[kb], NN)

        for b in range(model):
            part_ref[span, b * block : (b + 1) * block] = (acc_ref[b] * scale_out).astype(BF16)


def backward_kernel(
    scale_in, scale_out, tile, rows_ref, columns_ref, tok_ref, err_ref, pre_ref, up_ref, down_ref,
    gpart_ref, act_ref, dpre_ref, acc_ref, count_ref, place_ref,
):
    hidden, tok_count, block = pre_ref.shape
    model = acc_ref.shape[0]
    per_owner = gpart_ref.shape[2] // block
    order_blocks(columns_ref, count_ref, place_ref)

    @pl.loop(0, tok_count // tile)
    def _(i):
        span = pl.ds(pl.multiple_of(i * tile, tile), tile)
        acc_ref[...] = jnp.zeros_like(acc_ref)

        @pl.loop(0, hidden)
        def _(h):
            ka, kb = place_ref[2 * h], place_ref[2 * h + 1]
            ra, rb = rows_ref[ka], rows_ref[kb]
            ea = err_ref[span, pl.ds(pl.multiple_of(ra * block, block), block)]
            eb = err_ref[span, pl.ds(pl.multiple_of(rb * block, block), block)]
            dact = (dot(ea, down_ref[ka], NT) + dot(eb, down_ref[kb], NT)) * scale_out
            pre = pre_ref[h, span, :]
            sig = sigmoid(pre)
            act_ref[h, span, :] = (pre * sig).astype(BF16)
            dpre = (dact * sig * (1.0 + pre * (1.0 - sig))).astype(BF16)
            dpre_ref[h, span, :] = dpre
            acc_ref[ra] += dot(dpre, up_ref[ka], NT)
            acc_ref[rb] += dot(dpre, up_ref[kb], NT)

        for b in range(model):
            at = (b % per_owner) * block
            gpart_ref[b // per_owner, span, at : at + block] = (acc_ref[b] * scale_in).astype(BF16)


def weight_kernel(
    scale_in, scale_out, rows_ref, columns_ref, tok_ref, err_ref, act_ref, dpre_ref, up_ref, down_ref,
    up_half_ref, down_half_ref,
):
    blocks, block, _ = up_ref.shape

    @pl.loop(0, blocks)
    def _(k):
        h = columns_ref[k]
        features = pl.ds(pl.multiple_of(rows_ref[k] * block, block), block)
        grad_down = dot(act_ref[h], err_ref[:, features], TN)
        down_half_ref[k] = 0.5 * down_ref[k].astype(F32) - (STEP_RATE * scale_out) * grad_down
        grad_up = dot(tok_ref[:, features], dpre_ref[h], TN)
        up_half_ref[k] = 0.5 * up_ref[k].astype(F32) - (STEP_RATE * scale_in) * grad_up


def neighbours():
    dp, t = lax.axis_index("dp"), lax.axis_index("tensor")
    twin, across = (dp, t ^ 1), (dp, t ^ 2)
    barrier = pltpu.get_barrier_semaphore()
    for device in (twin, across):
        pl.semaphore_signal(barrier, inc=1, device_id=device, device_id_type=MESH)
    pl.semaphore_wait(barrier, 2)
    return t // 2, t % 2, twin, across


def send(src, dst, sems, kind, i, device):
    return pltpu.make_async_remote_copy(
        src_ref=src, dst_ref=dst, send_sem=sems.at[0, kind, i], recv_sem=sems.at[1, kind, i],
        device_id=device, device_id_type=MESH,
    )


def error_kernel(chunks, part_ref, target_ref, err_ref, from_twin, pair_sum, from_across, sems):
    half = from_twin.shape[0]
    step = half // chunks
    strip = 32
    _, core, twin, across = neighbours()
    mine, other = core * half, (1 - core) * half

    def at(base, i):
        return pl.ds(pl.multiple_of(base + i * step, step), step)

    def here(i):
        return pl.ds(i * step, step)

    to_twin = [send(part_ref.at[at(other, i)], from_twin.at[here(i)], sems, 0, i, twin) for i in range(chunks)]
    to_across = [send(pair_sum.at[here(i)], from_across.at[here(i)], sems, 1, i, across) for i in range(chunks)]
    share = [send(err_ref.at[at(mine, i)], err_ref.at[at(mine, i)], sems, 2, i, twin) for i in range(chunks)]
    for i in range(chunks):
        to_twin[i].start()
    for i in range(chunks):
        to_twin[i].wait_recv()

        @pl.loop(0, step // strip)
        def _(j):
            local = pl.ds(pl.multiple_of(i * step + j * strip, strip), strip)
            whole = pl.ds(pl.multiple_of(mine + i * step + j * strip, strip), strip)
            total = part_ref[whole, :].astype(F32) + from_twin[local, :].astype(F32)
            pair_sum[local, :] = total.astype(BF16)

        to_across[i].start()
    for i in range(chunks):
        to_across[i].wait_recv()

        @pl.loop(0, step // strip)
        def _(j):
            local = pl.ds(pl.multiple_of(i * step + j * strip, strip), strip)
            whole = pl.ds(pl.multiple_of(mine + i * step + j * strip, strip), strip)
            total = pair_sum[local, :].astype(F32) + from_across[local, :].astype(F32)
            err_ref[whole, :] = (total - target_ref[whole, :].astype(F32)).astype(BF16)

        share[i].start()
    for i in range(chunks):
        share[i].wait_recv()
    for i in range(chunks):
        to_twin[i].wait_send()
        to_across[i].wait_send()
        share[i].wait_send()


def scatter_kernel(chunks, gpart_ref, out_ref, from_twin, pair_sum, from_across, sems):
    tok_count = out_ref.shape[0]
    step = tok_count // chunks
    strip = 64
    chip, core, twin, across = neighbours()
    far = 1 - chip

    def here(i):
        return pl.ds(i * step, step)

    def to_twin(which, kind, i):
        return send(
            gpart_ref.at[2 * which + 1 - core, here(i)], from_twin.at[kind, here(i)], sems, kind, i, twin
        )

    sent_far = [to_twin(far, 0, i) for i in range(chunks)]
    sent_near = [to_twin(chip, 1, i) for i in range(chunks)]
    to_across = [send(pair_sum.at[here(i)], from_across.at[here(i)], sems, 2, i, across) for i in range(chunks)]
    for i in range(chunks):
        sent_far[i].start()
    for i in range(chunks):
        sent_near[i].start()
    for i in range(chunks):
        sent_far[i].wait_recv()

        @pl.loop(0, step // strip)
        def _(j):
            rows = pl.ds(pl.multiple_of(i * step + j * strip, strip), strip)
            total = gpart_ref[2 * far + core, rows, :].astype(F32) + from_twin[0, rows, :].astype(F32)
            pair_sum[rows, :] = total.astype(BF16)

        to_across[i].start()
    for i in range(chunks):
        sent_near[i].wait_recv()
        to_across[i].wait_recv()

        @pl.loop(0, step // strip)
        def _(j):
            rows = pl.ds(pl.multiple_of(i * step + j * strip, strip), strip)
            total = gpart_ref[2 * chip + core, rows, :].astype(F32) + from_twin[1, rows, :].astype(F32)
            out_ref[rows, :] = (total + from_across[rows, :].astype(F32)).astype(BF16)

    for i in range(chunks):
        sent_far[i].wait_send()
        sent_near[i].wait_send()
        to_across[i].wait_send()


SMEM_SPEC = pl.BlockSpec(memory_space=pltpu.SMEM)
VMEM_SPEC = pl.BlockSpec(memory_space=pltpu.VMEM)


def call(kernel, outs, scratch, indices, *arrays, **params):
    flops = params.pop("flops", 0)
    moved = sum(a.size * a.dtype.itemsize for a in (*arrays, *outs))
    return pl.pallas_call(
        kernel,
        out_shape=outs,
        in_specs=[SMEM_SPEC] * len(indices) + [VMEM_SPEC] * len(arrays),
        out_specs=[VMEM_SPEC] * len(outs),
        scratch_shapes=scratch,
        compiler_params=pltpu.CompilerParams(vmem_limit_bytes=56 << 20, **params),
        cost_estimate=pl.CostEstimate(flops=flops, bytes_accessed=moved, transcendentals=0),
    )(*indices, *arrays)


def on_device(tokens, targets, up_weight, down_weight, block_rows, block_columns):
    tok_count, width = tokens.shape
    up_local, down_local = up_weight[0], down_weight[0]
    blocks, block, _ = up_local.shape
    model = width // block
    tensor_count = lax.axis_size("tensor")
    hidden = H // (tensor_count * block)
    scale_in = (D // 4) ** (-0.5)
    scale_out = (H // 4) ** (-0.5)
    tile = 256
    pass_flops = 2 * tok_count * blocks * block * block
    apart = (lax.axis_size("dp").bit_length() - 1) // 2
    pairs = [(i, i ^ 1 << apart) for i in range(lax.axis_size("dp"))]
    indices = (block_rows, block_columns)
    place = [pltpu.SMEM((hidden,), jnp.int32), pltpu.SMEM((2 * hidden,), jnp.int32)]

    def array(*shape, dtype=BF16):
        return jax.ShapeDtypeStruct(shape, dtype)

    first, second = blocks // 4, blocks // 2
    chunks = 6

    def swap(x):
        return lax.ppermute(x, "dp", pairs)

    peer_up_a = swap(up_local[:first])
    pre, part = call(
        lambda *refs: forward_kernel(scale_in, scale_out, tile, *refs),
        [array(hidden, tok_count, block, dtype=F32), array(tok_count, width)],
        [pltpu.VMEM((model, tile, block), F32), *place],
        indices, tokens, up_local, down_local, flops=2 * pass_flops,
    )
    (err,) = call(
        lambda *refs: error_kernel(chunks, *refs),
        [array(tok_count, width)],
        [pltpu.VMEM((tok_count // 2, width), BF16)] * 3 + [pltpu.SemaphoreType.DMA((2, 3, chunks))],
        (), part, targets, collective_id=1, has_side_effects=True, flops=10 * pass_flops,
    )
    up_b, err = lax.optimization_barrier((up_local[first:second], err))
    peer_up_b = swap(up_b)
    gpart, act, dpre = call(
        lambda *refs: backward_kernel(scale_in, scale_out, tile, *refs),
        [array(tensor_count, tok_count, width // tensor_count), array(hidden, tok_count, block), array(hidden, tok_count, block)],
        [pltpu.VMEM((model, tile, block), F32), *place],
        indices, tokens, err, pre, up_local, down_local, flops=2 * pass_flops,
    )
    owned = (tok_count, width // tensor_count)
    (input_grad,) = call(
        lambda *refs: scatter_kernel(chunks, *refs),
        [array(*owned)],
        [pltpu.VMEM((2, *owned), BF16)] + [pltpu.VMEM(owned, BF16)] * 2 + [pltpu.SemaphoreType.DMA((2, 3, chunks))],
        (), gpart, collective_id=2, has_side_effects=True, flops=5 * pass_flops,
    )
    up_c, down_all, input_grad, act = lax.optimization_barrier((up_local[second:], down_local, input_grad, act))
    peer_up_c = swap(up_c)
    peer_down = swap(down_all)
    up_half, down_half = call(
        lambda *refs: weight_kernel(scale_in, scale_out, *refs),
        [array(blocks, block, block, dtype=F32)] * 2,
        [],
        indices, tokens, err, act, dpre, up_local, down_local, flops=2 * pass_flops,
    )
    peer_up = jnp.concatenate([peer_up_a, peer_up_b, peer_up_c], axis=0)
    new_up = (up_half + 0.5 * peer_up.astype(F32)).astype(BF16)
    new_down = (down_half + 0.5 * peer_down.astype(F32)).astype(BF16)
    return (new_up[None], new_down[None], input_grad)


def solution(mesh):
    return jax.shard_map(
        on_device,
        mesh=mesh,
        in_specs=(
            P("dp", None),
            P("dp", None),
            P("dp", "tensor", None, None),
            P("dp", "tensor", None, None),
            P("tensor"),
            P("tensor"),
        ),
        out_specs=(P("dp", "tensor", None, None), P("dp", "tensor", None, None), P("dp", "tensor")),
        check_vma=False,
    )
```

```python
import jax
import jax.numpy as jnp
from jax import lax
from jax.experimental import pallas as pl
from jax.experimental.pallas import tpu as pltpu
from jax.sharding import PartitionSpec as P

D = 2048
H = 8192
STEP_RATE = 0.5
MESH = pl.DeviceIdType.MESH
F32 = jnp.float32
BF16 = jnp.bfloat16
TILE = 128
PIECE = 2
EARLY = (2, 2, 1)


def dot(a, b, contract):
    return lax.dot_general(a, b, (contract, ((), ())), preferred_element_type=F32)


NN = ((1,), (0,))
NT = ((1,), (1,))
TN = ((0,), (0,))


def sigmoid(v):
    return 1.0 / (1.0 + jnp.exp(-v))


def equal(a, b):
    return 1 - jnp.minimum((a - b) * (a - b), 1)


def less(a, b):
    return jnp.clip(b - a, 0, 1)


def rank_blocks(values_ref, rank_ref):
    n = values_ref.shape[0]

    @pl.loop(0, n)
    def _(k):
        own = values_ref[k] * n + k
        rank = jnp.int32(0)
        for j in range(n):
            rank += less(values_ref[j] * n + j, own)
        rank_ref[k] = rank


def in_order(rank_ref, value, place_ref):
    n = rank_ref.shape[0]

    @pl.loop(0, n)
    def _(i):
        place = jnp.int32(0)
        for k in range(n):
            place += value(k) * equal(rank_ref[k], i)
        place_ref[i] = place


def step_kernel(
    apart, scale_in, scale_out,
    rows_ref, cols_ref, tok_hbm, target_hbm, up_hbm, down_hbm,
    new_up_hbm, new_down_hbm, grad_hbm,
    tok, target, up, down, pre, act, dpre, seg, part, err_mine, err_other, gpart,
    out_twin, out_sum, out_across, grad_twin, grad_sum, grad_across, grad,
    peer, up_half, down_half,
    rank, col_block, col_row, row_block, row_col, row_row, keep, slot,
    load_sem, weight_sem, out_sem, grad_sem, store_sem,
):
    hidden, tok_count, block = pre.shape
    blocks = up.shape[0]
    model = tok.shape[0]
    half = tok_count // 2
    steps = half // TILE
    pieces = blocks // PIECE

    dp, t = lax.axis_index("dp"), lax.axis_index("tensor")
    twin, across, partner = (dp, t ^ 1), (dp, t ^ 2), (dp ^ (1 << apart), t)
    chip, core = t // 2, t % 2
    far = 1 - chip
    mine, other = core * half, (1 - core) * half

    def aligned(start):
        return pl.multiple_of(start, TILE)

    loads = [
        pltpu.make_async_copy(up_hbm, up, load_sem.at[0]),
        *(
            pltpu.make_async_copy(tok_hbm.at[:, b * block : (b + 1) * block], tok.at[b], load_sem.at[3 + b])
            for b in range(model)
        ),
        pltpu.make_async_copy(down_hbm, down, load_sem.at[1]),
        pltpu.make_async_copy(target_hbm.at[pl.ds(aligned(mine), half)], target, load_sem.at[2]),
    ]
    for load in loads:
        load.start()

    barrier = pltpu.get_barrier_semaphore()
    for device in (twin, across, partner):
        pl.semaphore_signal(barrier, inc=1, device_id=device, device_id_type=MESH)
    pl.semaphore_wait(barrier, 3)

    def remote(src, dst, sems, where, device):
        return pltpu.make_async_remote_copy(
            src_ref=src, dst_ref=dst, send_sem=sems.at[(0, *where)], recv_sem=sems.at[(1, *where)],
            device_id=device, device_id_type=MESH,
        )

    def weights_to_partner(which, p):
        span = pl.ds(p * PIECE, PIECE)
        return remote((up_hbm, down_hbm)[which].at[span], peer.at[which, span], weight_sem, (which, p), partner)

    everything = [(which, p) for which in range(2) for p in range(pieces)]

    def send_pieces(first, last):
        for which, p in everything[first:last]:
            weights_to_partner(which, p).start()

    cut = [sum(EARLY[: i + 1]) for i in range(3)]
    send_pieces(0, cut[0])

    rank_blocks(cols_ref, rank)
    in_order(rank, lambda k: k, col_block)
    in_order(rank, lambda k: rows_ref[k], col_row)
    rank_blocks(rows_ref, rank)
    in_order(rank, lambda k: k, row_block)
    in_order(rank, lambda k: cols_ref[k], row_col)
    in_order(rank, lambda k: rows_ref[k], row_row)
    keep[0] = 0

    @pl.loop(1, blocks)
    def _(j):
        keep[j] = equal(row_row[j], row_row[j - 1])

    @pl.loop(0, model)
    def _(b):
        upto, here = jnp.int32(0), jnp.int32(0)
        for k in range(blocks):
            upto += less(rows_ref[k], b + 1)
            here += equal(rows_ref[k], b)
        slot[b] = upto * jnp.minimum(here, 1)

    seg[0] = jnp.zeros_like(seg[0])
    for load in loads[:-1]:
        load.wait()

    def sum_by_row(left, right, contract, span):
        @pl.loop(0, blocks)
        def _(j):
            product = dot(left[row_col[j], span, :], right[row_block[j]], contract)
            seg[j + 1] = product + seg[j] * keep[j].astype(F32)

    def forward(base):
        span = pl.ds(aligned(base), TILE)

        @pl.loop(0, hidden)
        def _(h):
            first, second = (
                dot(tok[col_row[2 * h + i], span, :], up[col_block[2 * h + i]], NN) for i in range(2)
            )
            v = (first + second) * scale_in
            pre[h, span, :] = v
            act[h, span, :] = (v * sigmoid(v)).astype(BF16)

        sum_by_row(act, down, NN, span)
        for b in range(model):
            part[span, b * block : (b + 1) * block] = (seg[slot[b]] * scale_out).astype(BF16)

    def backward(base, err, i):
        span, near = pl.ds(aligned(base + i * TILE), TILE), pl.ds(aligned(i * TILE), TILE)

        @pl.loop(0, hidden)
        def _(h):
            first, second = (
                dot(err[col_row[2 * h + n], near, :], down[col_block[2 * h + n]], NT) for n in range(2)
            )
            dact = (first + second) * scale_out
            v = pre[h, span, :]
            sig = sigmoid(v)
            dpre[h, span, :] = (dact * sig * (1.0 + v * (1.0 - sig))).astype(BF16)

        sum_by_row(dpre, up, NT, span)
        per_owner = gpart.shape[2] // block
        for b in range(model):
            at = (b % per_owner) * block
            gpart[b // per_owner, span, at : at + block] = (seg[slot[b]] * scale_in).astype(BF16)

    def rows(base, i):
        return pl.ds(aligned(base + i * TILE), TILE)

    def part_to_twin(i):
        return remote(part.at[rows(other, i)], out_twin.at[rows(0, i)], out_sem, (0, i), twin)

    def sum_to_across(i):
        return remote(out_sum.at[rows(0, i)], out_across.at[rows(0, i)], out_sem, (1, i), across)

    def error_to_twin(i):
        return remote(err_mine.at[:, rows(0, i)], err_other.at[:, rows(0, i)], out_sem, (2, i), twin)

    def grad_to_twin(which, base, i):
        owner = (far, chip)[which]
        q = base // TILE + i
        return remote(
            gpart.at[2 * owner + 1 - core, rows(base, i)], grad_twin.at[which, rows(base, i)], grad_sem, (which, q), twin
        )

    def grad_to_across(base, i):
        q = base // TILE + i
        return remote(grad_sum.at[rows(base, i)], grad_across.at[rows(base, i)], grad_sem, (2, q), across)

    def strips(size, body):
        @pl.loop(0, TILE // size)
        def _(s):
            body(s * size)

    @pl.loop(0, steps)
    def _(i):
        forward(other + i * TILE)
        part_to_twin(i).start()

    @pl.loop(0, steps)
    def _(i):
        forward(mine + i * TILE)
        part_to_twin(i).wait_recv()

        def body(s):
            local = pl.ds(pl.multiple_of(i * TILE + s, 32), 32)
            whole = pl.ds(pl.multiple_of(mine + i * TILE + s, 32), 32)
            out_sum[local, :] = (part[whole, :].astype(F32) + out_twin[local, :].astype(F32)).astype(BF16)

        strips(32, body)
        sum_to_across(i).start()

    send_pieces(cut[0], cut[1])
    loads[-1].wait()

    @pl.loop(0, steps)
    def _(i):
        sum_to_across(i).wait_recv()

        def body(s):
            local = pl.ds(pl.multiple_of(i * TILE + s, 32), 32)
            output = out_sum[local, :].astype(F32) + out_across[local, :].astype(F32)
            error = (output - target[local, :].astype(F32)).astype(BF16)
            for b in range(model):
                err_mine[b, local, :] = error[:, b * block : (b + 1) * block]

        strips(32, body)
        error_to_twin(i).start()
        backward(mine, err_mine, i)
        grad_to_twin(0, mine, i).start()
        grad_to_twin(1, mine, i).start()

    send_pieces(cut[1], cut[2])

    @pl.loop(0, steps)
    def _(i):
        error_to_twin(i).wait_recv()

    def pass_on(base, i):
        grad_to_twin(0, base, i).wait_recv()

        def body(s):
            whole = pl.ds(pl.multiple_of(base + i * TILE + s, 64), 64)
            total = gpart[2 * far + core, whole, :].astype(F32) + grad_twin[0, whole, :].astype(F32)
            grad_sum[whole, :] = total.astype(BF16)

        strips(64, body)
        grad_to_across(base, i).start()

    def finish(base, i):
        grad_to_twin(1, base, i).wait_recv()
        grad_to_across(base, i).wait_recv()

        def body(s):
            whole = pl.ds(pl.multiple_of(base + i * TILE + s, 64), 64)
            total = gpart[2 * chip + core, whole, :].astype(F32) + grad_twin[1, whole, :].astype(F32)
            grad[whole, :] = (total + grad_across[whole, :].astype(F32)).astype(BF16)

        strips(64, body)

    @pl.loop(0, steps)
    def _(i):
        backward(other, err_other, i)
        grad_to_twin(0, other, i).start()
        grad_to_twin(1, other, i).start()
        pass_on(other, i)
        pass_on(mine, i)

    send_pieces(cut[2], len(everything))

    @pl.loop(0, blocks)
    def _(k):
        h = cols_ref[k]
        grad_down = dot(act[h, pl.ds(aligned(mine), half), :], err_mine[rows_ref[k]], TN)
        grad_down += dot(act[h, pl.ds(aligned(other), half), :], err_other[rows_ref[k]], TN)
        down_half[k] = 0.5 * down[k].astype(F32) - (STEP_RATE * scale_out) * grad_down
        grad_up = dot(tok[rows_ref[k]], dpre[h], TN)
        up_half[k] = 0.5 * up[k].astype(F32) - (STEP_RATE * scale_in) * grad_up

    @pl.loop(0, steps)
    def _(i):
        finish(other, i)
        finish(mine, i)

    store_grad = pltpu.make_async_copy(grad, grad_hbm, store_sem.at[2, 0])
    store_grad.start()

    for which, (own, held, new_hbm) in enumerate(((up, up_half, new_up_hbm), (down, down_half, new_down_hbm))):

        @pl.loop(0, pieces)
        def _(p):
            weights_to_partner(which, p).wait_recv()
            for b in range(PIECE):
                k = p * PIECE + b
                own[k] = (held[k] + 0.5 * peer[which, k].astype(F32)).astype(BF16)
            span = pl.ds(p * PIECE, PIECE)
            pltpu.make_async_copy(own.at[span], new_hbm.at[span], store_sem.at[which, p]).start()

    store_grad.wait()
    for which, (own, new_hbm) in enumerate(((up, new_up_hbm), (down, new_down_hbm))):

        @pl.loop(0, pieces)
        def _(p):
            weights_to_partner(which, p).wait_send()
            span = pl.ds(p * PIECE, PIECE)
            pltpu.make_async_copy(own.at[span], new_hbm.at[span], store_sem.at[which, p]).wait()

    @pl.loop(0, steps)
    def _(i):
        part_to_twin(i).wait_send()
        sum_to_across(i).wait_send()
        error_to_twin(i).wait_send()
        for base in (mine, other):
            grad_to_twin(0, base, i).wait_send()
            grad_to_twin(1, base, i).wait_send()
            grad_to_across(base, i).wait_send()


def on_device(tokens, targets, up_weight, down_weight, block_rows, block_columns):
    tok_count, width = tokens.shape
    up_local, down_local = up_weight[0], down_weight[0]
    blocks, block, _ = up_local.shape
    model = width // block
    tensor_count = lax.axis_size("tensor")
    hidden = H // (tensor_count * block)
    scale_in = (D // 4) ** (-0.5)
    scale_out = (H // 4) ** (-0.5)
    apart = (lax.axis_size("dp").bit_length() - 1) // 2
    half, owned = tok_count // 2, width // tensor_count
    steps, pieces = half // TILE, blocks // PIECE
    vmem, dma = pltpu.VMEM, pltpu.SemaphoreType.DMA
    anywhere = pl.BlockSpec(memory_space=pl.ANY)
    scalars = pl.BlockSpec(memory_space=pltpu.SMEM)
    weights = jax.ShapeDtypeStruct((blocks, block, block), BF16)
    flops = 12 * tok_count * blocks * block * block
    new_up, new_down, input_grad = pl.pallas_call(
        lambda *refs: step_kernel(apart, scale_in, scale_out, *refs),
        out_shape=[weights, weights, jax.ShapeDtypeStruct((tok_count, owned), BF16)],
        in_specs=[scalars, scalars, anywhere, anywhere, anywhere, anywhere],
        out_specs=[anywhere, anywhere, anywhere],
        scratch_shapes=[
            vmem((model, tok_count, block), BF16),
            vmem((half, width), BF16),
            vmem((blocks, block, block), BF16),
            vmem((blocks, block, block), BF16),
            vmem((hidden, tok_count, block), F32),
            vmem((hidden, tok_count, block), BF16),
            vmem((hidden, tok_count, block), BF16),
            vmem((blocks + 1, TILE, block), F32),
            vmem((tok_count, width), BF16),
            vmem((model, half, block), BF16),
            vmem((model, half, block), BF16),
            vmem((tensor_count, tok_count, owned), BF16),
            vmem((half, width), BF16),
            vmem((half, width), BF16),
            vmem((half, width), BF16),
            vmem((2, tok_count, owned), BF16),
            vmem((tok_count, owned), BF16),
            vmem((tok_count, owned), BF16),
            vmem((tok_count, owned), BF16),
            vmem((2, blocks, block, block), BF16),
            vmem((blocks, block, block), F32),
            vmem((blocks, block, block), F32),
            *[pltpu.SMEM((blocks,), jnp.int32)] * 7,
            pltpu.SMEM((model,), jnp.int32),
            dma((3 + model,)),
            dma((2, 2, pieces)),
            dma((2, 3, steps)),
            dma((2, 3, 2 * steps)),
            dma((3, pieces)),
        ],
        compiler_params=pltpu.CompilerParams(
            collective_id=0, has_side_effects=True, vmem_limit_bytes=62 << 20
        ),
        cost_estimate=pl.CostEstimate(flops=flops, bytes_accessed=20 << 20, transcendentals=0),
    )(block_rows, block_columns, tokens, targets, up_local, down_local)
    return (new_up[None], new_down[None], input_grad)


def solution(mesh):
    return jax.shard_map(
        on_device,
        mesh=mesh,
        in_specs=(
            P("dp", None),
            P("dp", None),
            P("dp", "tensor", None, None),
            P("dp", "tensor", None, None),
            P("tensor"),
            P("tensor"),
        ),
        out_specs=(P("dp", "tensor", None, None), P("dp", "tensor", None, None), P("dp", "tensor")),
        check_vma=False,
    )
```

```python
import jax
import jax.numpy as jnp
from jax import lax
from jax.experimental import pallas as pl
from jax.experimental.pallas import tpu as pltpu
from jax.sharding import PartitionSpec as P

D = 2048
H = 8192
STEP_RATE = 0.5
MESH = pl.DeviceIdType.MESH
F32 = jnp.float32
BF16 = jnp.bfloat16
TILE = 128
PIECE = 2
VMEM_LIMIT = 54 << 20
STORES = 4
EARLY = (3, 3, 2)


def dot(a, b, contract):
    return lax.dot_general(a, b, (contract, ((), ())), preferred_element_type=F32)


NN = ((1,), (0,))
NT = ((1,), (1,))
TN = ((0,), (0,))


def sigmoid(v):
    return 1.0 / (1.0 + jnp.exp(-v))


def equal(a, b):
    return 1 - jnp.minimum((a - b) * (a - b), 1)


def less(a, b):
    return jnp.clip(b - a, 0, 1)


def rank_blocks(values_ref, rank_ref):
    n = values_ref.shape[0]

    @pl.loop(0, n)
    def _(k):
        own = values_ref[k] * n + k
        rank = jnp.int32(0)
        for j in range(n):
            rank += less(values_ref[j] * n + j, own)
        rank_ref[k] = rank


def in_order(rank_ref, value, place_ref):
    n = rank_ref.shape[0]

    @pl.loop(0, n)
    def _(i):
        place = jnp.int32(0)
        for k in range(n):
            place += value(k) * equal(rank_ref[k], i)
        place_ref[i] = place


def step_kernel(
    apart, scale_in, scale_out,
    rows_ref, cols_ref, tok_hbm, target_hbm, up_hbm, down_hbm,
    new_up, new_down, grad,
    tok, target, up, down, pre, act, dpre, seg, part, err_mine, err_other, gpart,
    out_twin, out_sum, out_across, grad_twin, grad_sum, grad_across,
    peer, down_half,
    rank, col_block, col_row, row_block, row_col, row_row, keep, slot,
    load_sem, weight_sem, out_sem, grad_sem,
):
    hidden, tok_count, block = pre.shape
    blocks = up.shape[0]
    model = tok.shape[0]
    half = tok_count // 2
    steps = half // TILE
    pieces = blocks // PIECE

    dp, t = lax.axis_index("dp"), lax.axis_index("tensor")
    twin, across, partner = (dp, t ^ 1), (dp, t ^ 2), (dp ^ (1 << apart), t)
    chip, core = t // 2, t % 2
    far = 1 - chip
    mine, other = core * half, (1 - core) * half

    def aligned(start):
        return pl.multiple_of(start, TILE)

    loads = [
        pltpu.make_async_copy(up_hbm, up, load_sem.at[0]),
        *(
            pltpu.make_async_copy(tok_hbm.at[:, b * block : (b + 1) * block], tok.at[b], load_sem.at[3 + b])
            for b in range(model)
        ),
        pltpu.make_async_copy(down_hbm, down, load_sem.at[1]),
        pltpu.make_async_copy(target_hbm.at[pl.ds(aligned(mine), half)], target, load_sem.at[2]),
    ]
    for load in loads:
        load.start()

    barrier = pltpu.get_barrier_semaphore()
    for device in (twin, across, partner):
        pl.semaphore_signal(barrier, inc=1, device_id=device, device_id_type=MESH)
    pl.semaphore_wait(barrier, 3)

    def remote(src, dst, sems, where, device):
        return pltpu.make_async_remote_copy(
            src_ref=src, dst_ref=dst, send_sem=sems.at[(0, *where)], recv_sem=sems.at[(1, *where)],
            device_id=device, device_id_type=MESH,
        )

    def weights_to_partner(which, p):
        span = pl.ds(p * PIECE, PIECE)
        return remote((up_hbm, down_hbm)[which].at[span], peer.at[which, span], weight_sem, (which, p), partner)

    everything = [(which, p) for which in range(2) for p in range(pieces)]

    def send_pieces(first, last):
        for which, p in everything[first:last]:
            weights_to_partner(which, p).start()

    cut = [sum(EARLY[: i + 1]) for i in range(3)]
    send_pieces(0, cut[0])

    rank_blocks(cols_ref, rank)
    in_order(rank, lambda k: k, col_block)
    in_order(rank, lambda k: rows_ref[k], col_row)
    rank_blocks(rows_ref, rank)
    in_order(rank, lambda k: k, row_block)
    in_order(rank, lambda k: cols_ref[k], row_col)
    in_order(rank, lambda k: rows_ref[k], row_row)
    keep[0] = 0

    @pl.loop(1, blocks)
    def _(j):
        keep[j] = equal(row_row[j], row_row[j - 1])

    @pl.loop(0, model)
    def _(b):
        upto, here = jnp.int32(0), jnp.int32(0)
        for k in range(blocks):
            upto += less(rows_ref[k], b + 1)
            here += equal(rows_ref[k], b)
        slot[b] = upto * jnp.minimum(here, 1)

    seg[0] = jnp.zeros_like(seg[0])
    for load in loads[:-1]:
        load.wait()

    def sum_by_row(left, right, contract, span):
        @pl.loop(0, blocks)
        def _(j):
            product = dot(left[row_col[j], span, :], right[row_block[j]], contract)
            seg[j + 1] = product + seg[j] * keep[j].astype(F32)

    def forward(base):
        span = pl.ds(aligned(base), TILE)

        @pl.loop(0, hidden)
        def _(h):
            first, second = (
                dot(tok[col_row[2 * h + i], span, :], up[col_block[2 * h + i]], NN) for i in range(2)
            )
            v = (first + second) * scale_in
            pre[h, span, :] = v
            act[h, span, :] = (v * sigmoid(v)).astype(BF16)

        sum_by_row(act, down, NN, span)
        for b in range(model):
            part[span, b * block : (b + 1) * block] = (seg[slot[b]] * scale_out).astype(BF16)

    def backward(base, err, i):
        span, near = pl.ds(aligned(base + i * TILE), TILE), pl.ds(aligned(i * TILE), TILE)

        @pl.loop(0, hidden)
        def _(h):
            first, second = (
                dot(err[col_row[2 * h + n], near, :], down[col_block[2 * h + n]], NT) for n in range(2)
            )
            dact = (first + second) * scale_out
            v = pre[h, span, :]
            sig = sigmoid(v)
            dpre[h, span, :] = (dact * sig * (1.0 + v * (1.0 - sig))).astype(BF16)

        sum_by_row(dpre, up, NT, span)
        per_owner = gpart.shape[2] // block
        for b in range(model):
            at = (b % per_owner) * block
            gpart[b // per_owner, span, at : at + block] = (seg[slot[b]] * scale_in).astype(BF16)

    def up_half(k):
        return pre.at[k // 2, pl.ds(pl.multiple_of((k % 2) * block, block), block)]

    def rows(base, i):
        return pl.ds(aligned(base + i * TILE), TILE)

    def part_to_twin(i):
        return remote(part.at[rows(other, i)], out_twin.at[rows(0, i)], out_sem, (0, i), twin)

    def sum_to_across(i):
        return remote(out_sum.at[rows(0, i)], out_across.at[rows(0, i)], out_sem, (1, i), across)

    def error_to_twin(i):
        return remote(err_mine.at[:, rows(0, i)], err_other.at[:, rows(0, i)], out_sem, (2, i), twin)

    def grad_to_twin(which, base, i):
        owner = (far, chip)[which]
        q = base // TILE + i
        return remote(
            gpart.at[2 * owner + 1 - core, rows(base, i)], grad_twin.at[which, rows(base, i)], grad_sem, (which, q), twin
        )

    def grad_to_across(base, i):
        q = base // TILE + i
        return remote(grad_sum.at[rows(base, i)], grad_across.at[rows(base, i)], grad_sem, (2, q), across)

    def strips(size, body):
        @pl.loop(0, TILE // size)
        def _(s):
            body(s * size)

    @pl.loop(0, steps)
    def _(i):
        forward(other + i * TILE)
        part_to_twin(i).start()

    @pl.loop(0, steps)
    def _(i):
        forward(mine + i * TILE)
        part_to_twin(i).wait_recv()

        def body(s):
            local = pl.ds(pl.multiple_of(i * TILE + s, 32), 32)
            whole = pl.ds(pl.multiple_of(mine + i * TILE + s, 32), 32)
            out_sum[local, :] = (part[whole, :].astype(F32) + out_twin[local, :].astype(F32)).astype(BF16)

        strips(32, body)
        sum_to_across(i).start()

    send_pieces(cut[0], cut[1])
    loads[-1].wait()

    @pl.loop(0, steps)
    def _(i):
        sum_to_across(i).wait_recv()

        def body(s):
            local = pl.ds(pl.multiple_of(i * TILE + s, 32), 32)
            output = out_sum[local, :].astype(F32) + out_across[local, :].astype(F32)
            error = (output - target[local, :].astype(F32)).astype(BF16)
            for b in range(model):
                err_mine[b, local, :] = error[:, b * block : (b + 1) * block]

        strips(32, body)
        error_to_twin(i).start()
        backward(mine, err_mine, i)
        grad_to_twin(0, mine, i).start()
        grad_to_twin(1, mine, i).start()

    send_pieces(cut[1], cut[2])

    @pl.loop(0, steps)
    def _(i):
        error_to_twin(i).wait_recv()

    def pass_on(base, i):
        grad_to_twin(0, base, i).wait_recv()

        def body(s):
            whole = pl.ds(pl.multiple_of(base + i * TILE + s, 64), 64)
            total = gpart[2 * far + core, whole, :].astype(F32) + grad_twin[0, whole, :].astype(F32)
            grad_sum[whole, :] = total.astype(BF16)

        strips(64, body)
        grad_to_across(base, i).start()

    def finish(base, i):
        grad_to_twin(1, base, i).wait_recv()
        grad_to_across(base, i).wait_recv()

        def body(s):
            whole = pl.ds(pl.multiple_of(base + i * TILE + s, 64), 64)
            total = gpart[2 * chip + core, whole, :].astype(F32) + grad_twin[1, whole, :].astype(F32)
            grad[whole, :] = (total + grad_across[whole, :].astype(F32)).astype(BF16)

        strips(64, body)

    @pl.loop(0, steps)
    def _(i):
        backward(other, err_other, i)
        grad_to_twin(0, other, i).start()
        grad_to_twin(1, other, i).start()
        pass_on(other, i)
        pass_on(mine, i)

    send_pieces(cut[2], len(everything))

    @pl.loop(0, blocks)
    def _(k):
        h = cols_ref[k]
        grad_down = dot(act[h, pl.ds(aligned(mine), half), :], err_mine[rows_ref[k]], TN)
        grad_down += dot(act[h, pl.ds(aligned(other), half), :], err_other[rows_ref[k]], TN)
        down_half[k] = 0.5 * down[k].astype(F32) - (STEP_RATE * scale_out) * grad_down
        grad_up = dot(tok[rows_ref[k]], dpre[h], TN)
        up_half(k)[...] = 0.5 * up[k].astype(F32) - (STEP_RATE * scale_in) * grad_up

    @pl.loop(0, steps)
    def _(i):
        finish(other, i)
        finish(mine, i)

    for which, (held, new) in enumerate(((up_half, new_up), (lambda k: down_half.at[k], new_down))):

        @pl.loop(0, pieces)
        def _(p):
            weights_to_partner(which, p).wait_recv()
            for b in range(PIECE):
                k = p * PIECE + b
                new[k] = (held(k)[...] + 0.5 * peer[which, k].astype(F32)).astype(BF16)

        @pl.loop(0, pieces)
        def _(p):
            weights_to_partner(which, p).wait_send()

    @pl.loop(0, steps)
    def _(i):
        part_to_twin(i).wait_send()
        sum_to_across(i).wait_send()
        error_to_twin(i).wait_send()
        for base in (mine, other):
            grad_to_twin(0, base, i).wait_send()
            grad_to_twin(1, base, i).wait_send()
            grad_to_across(base, i).wait_send()


def store_kernel(*refs):
    sources, targets, sems = refs[:3], refs[3:6], refs[6]
    copies = []
    for i, (source, target) in enumerate(zip(sources, targets)):
        size = source.shape[0] // STORES
        for j in range(STORES):
            span = pl.ds(j * size, size)
            copies.append(pltpu.make_async_copy(source.at[span], target.at[span], sems.at[i, j]))
    for copy in copies:
        copy.start()
    for copy in copies:
        copy.wait()


def on_device(tokens, targets, up_weight, down_weight, block_rows, block_columns):
    tok_count, width = tokens.shape
    up_local, down_local = up_weight[0], down_weight[0]
    blocks, block, _ = up_local.shape
    model = width // block
    tensor_count = lax.axis_size("tensor")
    hidden = H // (tensor_count * block)
    scale_in = (D // 4) ** (-0.5)
    scale_out = (H // 4) ** (-0.5)
    apart = (lax.axis_size("dp").bit_length() - 1) // 2
    half, owned = tok_count // 2, width // tensor_count
    steps, pieces = half // TILE, blocks // PIECE
    vmem, dma = pltpu.VMEM, pltpu.SemaphoreType.DMA
    anywhere = pl.BlockSpec(memory_space=pl.ANY)
    scalars = pl.BlockSpec(memory_space=pltpu.SMEM)
    weights = vmem((blocks, block, block), BF16)
    flops = 12 * tok_count * blocks * block * block
    new_up, new_down, input_grad = pl.pallas_call(
        lambda *refs: step_kernel(apart, scale_in, scale_out, *refs),
        out_shape=[weights, weights, vmem((tok_count, owned), BF16)],
        in_specs=[scalars, scalars, anywhere, anywhere, anywhere, anywhere],
        out_specs=[pl.BlockSpec(memory_space=vmem)] * 3,
        scratch_shapes=[
            vmem((model, tok_count, block), BF16),
            vmem((half, width), BF16),
            vmem((blocks, block, block), BF16),
            vmem((blocks, block, block), BF16),
            vmem((hidden, tok_count, block), F32),
            vmem((hidden, tok_count, block), BF16),
            vmem((hidden, tok_count, block), BF16),
            vmem((blocks + 1, TILE, block), F32),
            vmem((tok_count, width), BF16),
            vmem((model, half, block), BF16),
            vmem((model, half, block), BF16),
            vmem((tensor_count, tok_count, owned), BF16),
            vmem((half, width), BF16),
            vmem((half, width), BF16),
            vmem((half, width), BF16),
            vmem((2, tok_count, owned), BF16),
            vmem((tok_count, owned), BF16),
            vmem((tok_count, owned), BF16),
            vmem((2, blocks, block, block), BF16),
            vmem((blocks, block, block), F32),
            *[pltpu.SMEM((blocks,), jnp.int32)] * 7,
            pltpu.SMEM((model,), jnp.int32),
            dma((3 + model,)),
            dma((2, 2, pieces)),
            dma((2, 3, steps)),
            dma((2, 3, 2 * steps)),
        ],
        compiler_params=pltpu.CompilerParams(
            collective_id=0, has_side_effects=True, vmem_limit_bytes=VMEM_LIMIT
        ),
        cost_estimate=pl.CostEstimate(flops=flops, bytes_accessed=20 << 20, transcendentals=0),
    )(block_rows, block_columns, tokens, targets, up_local, down_local)
    new_up, new_down, input_grad = pl.pallas_call(
        store_kernel,
        out_shape=[jax.ShapeDtypeStruct(a.shape, a.dtype) for a in (new_up, new_down, input_grad)],
        in_specs=[pl.BlockSpec(memory_space=vmem)] * 3,
        out_specs=[anywhere] * 3,
        scratch_shapes=[dma((3, STORES))],
        compiler_params=pltpu.CompilerParams(vmem_limit_bytes=1 << 20),
        cost_estimate=pl.CostEstimate(flops=0, bytes_accessed=10 << 20, transcendentals=0),
    )(new_up, new_down, input_grad)
    return (new_up[None], new_down[None], input_grad)


def solution(mesh):
    return jax.shard_map(
        on_device,
        mesh=mesh,
        in_specs=(
            P("dp", None),
            P("dp", None),
            P("dp", "tensor", None, None),
            P("dp", "tensor", None, None),
            P("tensor"),
            P("tensor"),
        ),
        out_specs=(P("dp", "tensor", None, None), P("dp", "tensor", None, None), P("dp", "tensor")),
        check_vma=False,
    )
```

```python
import jax
import jax.numpy as jnp
from jax import lax
from jax.experimental import pallas as pl
from jax.experimental.pallas import tpu as pltpu
from jax.sharding import PartitionSpec as P

D = 2048
H = 8192
STEP_RATE = 0.5
MESH = pl.DeviceIdType.MESH
F32 = jnp.float32
BF16 = jnp.bfloat16
TILE = 128
PIECE = 2
VMEM_LIMIT = 54 << 20
STORES = 4
EARLY = (3, 5, 3)


def dot(a, b, contract):
    return lax.dot_general(a, b, (contract, ((), ())), preferred_element_type=F32)


NN = ((1,), (0,))
NT = ((1,), (1,))
TN = ((0,), (0,))


def sigmoid(v):
    return 1.0 / (1.0 + jnp.exp(-v))


def equal(a, b):
    return 1 - jnp.minimum((a - b) * (a - b), 1)


def less(a, b):
    return jnp.clip(b - a, 0, 1)


def rank_blocks(values_ref, rank_ref):
    n = values_ref.shape[0]

    @pl.loop(0, n)
    def _(k):
        own = values_ref[k] * n + k
        rank = jnp.int32(0)
        for j in range(n):
            rank += less(values_ref[j] * n + j, own)
        rank_ref[k] = rank


def in_order(rank_ref, value, place_ref):
    n = rank_ref.shape[0]

    @pl.loop(0, n)
    def _(i):
        place = jnp.int32(0)
        for k in range(n):
            place += value(k) * equal(rank_ref[k], i)
        place_ref[i] = place


def step_kernel(
    apart, scale_in, scale_out,
    rows_ref, cols_ref, tok_hbm, target_hbm, up_hbm, down_hbm,
    new_up, new_down, grad,
    tok, target, up, down, pre, act, dpre, seg, part, err_mine, err_other, gpart,
    out_twin, out_sum, out_across, grad_twin, grad_sum, grad_across,
    peer, down_half,
    rank, col_block, col_row, row_block, row_col, row_row, keep, slot,
    load_sem, weight_sem, out_sem, grad_sem,
):
    hidden, tok_count, block = pre.shape
    blocks = up.shape[0]
    model = tok.shape[0]
    half = tok_count // 2
    steps = half // TILE
    pieces = blocks // PIECE

    dp, t = lax.axis_index("dp"), lax.axis_index("tensor")
    twin, across, partner = (dp, t ^ 1), (dp, t ^ 2), (dp ^ (1 << apart), t)
    chip, core = t // 2, t % 2
    far = 1 - chip
    mine, other = core * half, (1 - core) * half

    def aligned(start):
        return pl.multiple_of(start, TILE)

    loads = [
        pltpu.make_async_copy(up_hbm, up, load_sem.at[0]),
        *(
            pltpu.make_async_copy(tok_hbm.at[:, b * block : (b + 1) * block], tok.at[b], load_sem.at[3 + b])
            for b in range(model)
        ),
        pltpu.make_async_copy(down_hbm, down, load_sem.at[1]),
        pltpu.make_async_copy(target_hbm.at[pl.ds(aligned(mine), half)], target, load_sem.at[2]),
    ]
    barrier = pltpu.get_barrier_semaphore()
    for device in (partner, across, twin):
        pl.semaphore_signal(barrier, inc=1, device_id=device, device_id_type=MESH)
    for load in loads:
        load.start()
    pl.semaphore_wait(barrier, 3)

    def remote(src, dst, sems, where, device):
        return pltpu.make_async_remote_copy(
            src_ref=src, dst_ref=dst, send_sem=sems.at[(0, *where)], recv_sem=sems.at[(1, *where)],
            device_id=device, device_id_type=MESH,
        )

    def weights_to_partner(which, p):
        span = pl.ds(p * PIECE, PIECE)
        return remote((up_hbm, down_hbm)[which].at[span], peer.at[which, span], weight_sem, (which, p), partner)

    everything = [(which, p) for which in range(2) for p in range(pieces)]

    def send_pieces(first, last):
        for which, p in everything[first:last]:
            weights_to_partner(which, p).start()

    cut = [sum(EARLY[: i + 1]) for i in range(3)]
    send_pieces(0, cut[0])

    rank_blocks(cols_ref, rank)
    in_order(rank, lambda k: k, col_block)
    in_order(rank, lambda k: rows_ref[k], col_row)
    rank_blocks(rows_ref, rank)
    in_order(rank, lambda k: k, row_block)
    in_order(rank, lambda k: cols_ref[k], row_col)
    in_order(rank, lambda k: rows_ref[k], row_row)
    keep[0] = 0

    @pl.loop(1, blocks)
    def _(j):
        keep[j] = equal(row_row[j], row_row[j - 1])

    @pl.loop(0, model)
    def _(b):
        upto, here = jnp.int32(0), jnp.int32(0)
        for k in range(blocks):
            upto += less(rows_ref[k], b + 1)
            here += equal(rows_ref[k], b)
        slot[b] = upto * jnp.minimum(here, 1)

    seg[0] = jnp.zeros_like(seg[0])
    for load in loads[:-1]:
        load.wait()

    def sum_by_row(left, right, contract, span):
        @pl.loop(0, blocks)
        def _(j):
            product = dot(left[row_col[j], span, :], right[row_block[j]], contract)
            seg[j + 1] = product + seg[j] * keep[j].astype(F32)

    def forward(base):
        span = pl.ds(aligned(base), TILE)

        @pl.loop(0, hidden)
        def _(h):
            first, second = (
                dot(tok[col_row[2 * h + i], span, :], up[col_block[2 * h + i]], NN) for i in range(2)
            )
            v = (first + second) * scale_in
            pre[h, span, :] = v
            act[h, span, :] = (v * sigmoid(v)).astype(BF16)

        sum_by_row(act, down, NN, span)
        for b in range(model):
            part[span, b * block : (b + 1) * block] = (seg[slot[b]] * scale_out).astype(BF16)

    def backward(base, err, i):
        span, near = pl.ds(aligned(base + i * TILE), TILE), pl.ds(aligned(i * TILE), TILE)

        @pl.loop(0, hidden)
        def _(h):
            first, second = (
                dot(err[col_row[2 * h + n], near, :], down[col_block[2 * h + n]], NT) for n in range(2)
            )
            dact = (first + second) * scale_out
            v = pre[h, span, :]
            sig = sigmoid(v)
            dpre[h, span, :] = (dact * sig * (1.0 + v * (1.0 - sig))).astype(BF16)

        sum_by_row(dpre, up, NT, span)
        per_owner = gpart.shape[2] // block
        for b in range(model):
            at = (b % per_owner) * block
            gpart[b // per_owner, span, at : at + block] = (seg[slot[b]] * scale_in).astype(BF16)

    def up_half(k):
        return pre.at[k // 2, pl.ds(pl.multiple_of((k % 2) * block, block), block)]

    def rows(base, i):
        return pl.ds(aligned(base + i * TILE), TILE)

    def part_to_twin(i):
        return remote(part.at[rows(other, i)], out_twin.at[rows(0, i)], out_sem, (0, i), twin)

    def sum_to_across(i):
        return remote(out_sum.at[rows(0, i)], out_across.at[rows(0, i)], out_sem, (1, i), across)

    def error_to_twin(i):
        return remote(err_mine.at[:, rows(0, i)], err_other.at[:, rows(0, i)], out_sem, (2, i), twin)

    def grad_to_twin(which, base, i):
        owner = (far, chip)[which]
        q = base // TILE + i
        return remote(
            gpart.at[2 * owner + 1 - core, rows(base, i)], grad_twin.at[which, rows(base, i)], grad_sem, (which, q), twin
        )

    def grad_to_across(base, i):
        q = base // TILE + i
        return remote(grad_sum.at[rows(base, i)], grad_across.at[rows(base, i)], grad_sem, (2, q), across)

    def strips(size, body):
        @pl.loop(0, TILE // size)
        def _(s):
            body(s * size)

    @pl.loop(0, steps)
    def _(i):
        forward(other + i * TILE)
        part_to_twin(i).start()

    @pl.loop(0, steps)
    def _(i):
        forward(mine + i * TILE)
        part_to_twin(i).wait_recv()

        def body(s):
            local = pl.ds(pl.multiple_of(i * TILE + s, 32), 32)
            whole = pl.ds(pl.multiple_of(mine + i * TILE + s, 32), 32)
            out_sum[local, :] = (part[whole, :].astype(F32) + out_twin[local, :].astype(F32)).astype(BF16)

        strips(32, body)
        sum_to_across(i).start()

    send_pieces(cut[0], cut[1])
    loads[-1].wait()

    @pl.loop(0, steps)
    def _(i):
        sum_to_across(i).wait_recv()

        def body(s):
            local = pl.ds(pl.multiple_of(i * TILE + s, 32), 32)
            output = out_sum[local, :].astype(F32) + out_across[local, :].astype(F32)
            error = (output - target[local, :].astype(F32)).astype(BF16)
            for b in range(model):
                err_mine[b, local, :] = error[:, b * block : (b + 1) * block]

        strips(32, body)
        error_to_twin(i).start()
        backward(mine, err_mine, i)
        grad_to_twin(0, mine, i).start()
        grad_to_twin(1, mine, i).start()

    send_pieces(cut[1], cut[2])

    @pl.loop(0, steps)
    def _(i):
        error_to_twin(i).wait_recv()

    def pass_on(base, i):
        grad_to_twin(0, base, i).wait_recv()

        def body(s):
            whole = pl.ds(pl.multiple_of(base + i * TILE + s, 64), 64)
            total = gpart[2 * far + core, whole, :].astype(F32) + grad_twin[0, whole, :].astype(F32)
            grad_sum[whole, :] = total.astype(BF16)

        strips(64, body)
        grad_to_across(base, i).start()

    def finish(base, i):
        grad_to_twin(1, base, i).wait_recv()
        grad_to_across(base, i).wait_recv()

        def body(s):
            whole = pl.ds(pl.multiple_of(base + i * TILE + s, 64), 64)
            total = gpart[2 * chip + core, whole, :].astype(F32) + grad_twin[1, whole, :].astype(F32)
            grad[whole, :] = (total + grad_across[whole, :].astype(F32)).astype(BF16)

        strips(64, body)

    @pl.loop(0, steps)
    def _(i):
        backward(other, err_other, i)
        grad_to_twin(0, other, i).start()
        grad_to_twin(1, other, i).start()
        pass_on(other, i)
        pass_on(mine, i)

    send_pieces(cut[2], len(everything))

    @pl.loop(0, blocks)
    def _(k):
        h = cols_ref[k]
        grad_down = dot(act[h, pl.ds(aligned(mine), half), :], err_mine[rows_ref[k]], TN)
        grad_down += dot(act[h, pl.ds(aligned(other), half), :], err_other[rows_ref[k]], TN)
        down_half[k] = 0.5 * down[k].astype(F32) - (STEP_RATE * scale_out) * grad_down
        grad_up = dot(tok[rows_ref[k]], dpre[h], TN)
        up_half(k)[...] = 0.5 * up[k].astype(F32) - (STEP_RATE * scale_in) * grad_up

    @pl.loop(0, steps)
    def _(i):
        finish(other, i)
        finish(mine, i)

    for which, (held, new) in enumerate(((up_half, new_up), (lambda k: down_half.at[k], new_down))):

        @pl.loop(0, pieces)
        def _(p):
            weights_to_partner(which, p).wait_recv()
            for b in range(PIECE):
                k = p * PIECE + b
                new[k] = (held(k)[...] + 0.5 * peer[which, k].astype(F32)).astype(BF16)

        @pl.loop(0, pieces)
        def _(p):
            weights_to_partner(which, p).wait_send()

    @pl.loop(0, steps)
    def _(i):
        part_to_twin(i).wait_send()
        sum_to_across(i).wait_send()
        error_to_twin(i).wait_send()
        for base in (mine, other):
            grad_to_twin(0, base, i).wait_send()
            grad_to_twin(1, base, i).wait_send()
            grad_to_across(base, i).wait_send()


def store_kernel(*refs):
    sources, targets, sems = refs[:3], refs[3:6], refs[6]
    copies = []
    for i, (source, target) in enumerate(zip(sources, targets)):
        size = source.shape[0] // STORES
        for j in range(STORES):
            span = pl.ds(j * size, size)
            copies.append(pltpu.make_async_copy(source.at[span], target.at[span], sems.at[i, j]))
    for copy in copies:
        copy.start()
    for copy in copies:
        copy.wait()


def on_device(tokens, targets, up_weight, down_weight, block_rows, block_columns):
    tok_count, width = tokens.shape
    up_local, down_local = up_weight[0], down_weight[0]
    blocks, block, _ = up_local.shape
    model = width // block
    tensor_count = lax.axis_size("tensor")
    hidden = H // (tensor_count * block)
    scale_in = (D // 4) ** (-0.5)
    scale_out = (H // 4) ** (-0.5)
    apart = (lax.axis_size("dp").bit_length() - 1) // 2
    half, owned = tok_count // 2, width // tensor_count
    steps, pieces = half // TILE, blocks // PIECE
    vmem, dma = pltpu.VMEM, pltpu.SemaphoreType.DMA
    anywhere = pl.BlockSpec(memory_space=pl.ANY)
    scalars = pl.BlockSpec(memory_space=pltpu.SMEM)
    weights = vmem((blocks, block, block), BF16)
    flops = 12 * tok_count * blocks * block * block
    new_up, new_down, input_grad = pl.pallas_call(
        lambda *refs: step_kernel(apart, scale_in, scale_out, *refs),
        out_shape=[weights, weights, vmem((tok_count, owned), BF16)],
        in_specs=[scalars, scalars, anywhere, anywhere, anywhere, anywhere],
        out_specs=[pl.BlockSpec(memory_space=vmem)] * 3,
        scratch_shapes=[
            vmem((model, tok_count, block), BF16),
            vmem((half, width), BF16),
            vmem((blocks, block, block), BF16),
            vmem((blocks, block, block), BF16),
            vmem((hidden, tok_count, block), F32),
            vmem((hidden, tok_count, block), BF16),
            vmem((hidden, tok_count, block), BF16),
            vmem((blocks + 1, TILE, block), F32),
            vmem((tok_count, width), BF16),
            vmem((model, half, block), BF16),
            vmem((model, half, block), BF16),
            vmem((tensor_count, tok_count, owned), BF16),
            vmem((half, width), BF16),
            vmem((half, width), BF16),
            vmem((half, width), BF16),
            vmem((2, tok_count, owned), BF16),
            vmem((tok_count, owned), BF16),
            vmem((tok_count, owned), BF16),
            vmem((2, blocks, block, block), BF16),
            vmem((blocks, block, block), F32),
            *[pltpu.SMEM((blocks,), jnp.int32)] * 7,
            pltpu.SMEM((model,), jnp.int32),
            dma((3 + model,)),
            dma((2, 2, pieces)),
            dma((2, 3, steps)),
            dma((2, 3, 2 * steps)),
        ],
        compiler_params=pltpu.CompilerParams(
            collective_id=0, has_side_effects=True, vmem_limit_bytes=VMEM_LIMIT
        ),
        cost_estimate=pl.CostEstimate(flops=flops, bytes_accessed=20 << 20, transcendentals=0),
    )(block_rows, block_columns, tokens, targets, up_local, down_local)
    new_up, new_down, input_grad = pl.pallas_call(
        store_kernel,
        out_shape=[jax.ShapeDtypeStruct(a.shape, a.dtype) for a in (new_up, new_down, input_grad)],
        in_specs=[pl.BlockSpec(memory_space=vmem)] * 3,
        out_specs=[anywhere] * 3,
        scratch_shapes=[dma((3, STORES))],
        compiler_params=pltpu.CompilerParams(vmem_limit_bytes=1 << 20),
        cost_estimate=pl.CostEstimate(flops=0, bytes_accessed=10 << 20, transcendentals=0),
    )(new_up, new_down, input_grad)
    return (new_up[None], new_down[None], input_grad)


def solution(mesh):
    return jax.shard_map(
        on_device,
        mesh=mesh,
        in_specs=(
            P("dp", None),
            P("dp", None),
            P("dp", "tensor", None, None),
            P("dp", "tensor", None, None),
            P("tensor"),
            P("tensor"),
        ),
        out_specs=(P("dp", "tensor", None, None), P("dp", "tensor", None, None), P("dp", "tensor")),
        check_vma=False,
    )
```

```python
import jax
import jax.numpy as jnp
from jax import lax
from jax.experimental import pallas as pl
from jax.experimental.pallas import tpu as pltpu
from jax.sharding import PartitionSpec as P

D = 2048
H = 8192
STEP_RATE = 0.5
MESH = pl.DeviceIdType.MESH
F32 = jnp.float32
BF16 = jnp.bfloat16
TILE = 128
PIECE = 2
VMEM_LIMIT = 54 << 20
STORES = 4
EARLY = (4, 5, 3)


def dot(a, b, contract):
    return lax.dot_general(a, b, (contract, ((), ())), preferred_element_type=F32)


NN = ((1,), (0,))
NT = ((1,), (1,))
TN = ((0,), (0,))


def sigmoid(v):
    return 1.0 / (1.0 + jnp.exp(-v))


def equal(a, b):
    return 1 - jnp.minimum((a - b) * (a - b), 1)


def less(a, b):
    return jnp.clip(b - a, 0, 1)


def rank_blocks(values_ref, rank_ref):
    n = values_ref.shape[0]

    @pl.loop(0, n)
    def _(k):
        own = values_ref[k] * n + k
        rank = jnp.int32(0)
        for j in range(n):
            rank += less(values_ref[j] * n + j, own)
        rank_ref[k] = rank


def in_order(rank_ref, value, place_ref):
    n = rank_ref.shape[0]

    @pl.loop(0, n)
    def _(i):
        place = jnp.int32(0)
        for k in range(n):
            place += value(k) * equal(rank_ref[k], i)
        place_ref[i] = place


def step_kernel(
    apart, scale_in, scale_out,
    rows_hbm, cols_hbm, tok_hbm, target_hbm, up_hbm, down_hbm,
    new_up, new_down, grad,
    tok, target, up, down, pre, act, dpre, seg, part, err_mine, err_other, gpart,
    out_twin, out_sum, out_across, grad_twin, grad_sum, grad_across,
    peer, down_half,
    rows_ref, cols_ref, rank, col_block, col_row, row_block, row_col, row_row, keep, slot,
    load_sem, weight_sem, out_sem, grad_sem,
):
    hidden, tok_count, block = pre.shape
    blocks = up.shape[0]
    model = tok.shape[0]
    half = tok_count // 2
    steps = half // TILE
    pieces = blocks // PIECE

    dp, t = lax.axis_index("dp"), lax.axis_index("tensor")
    twin, across, partner = (dp, t ^ 1), (dp, t ^ 2), (dp ^ (1 << apart), t)
    chip, core = t // 2, t % 2
    far = 1 - chip
    mine, other = core * half, (1 - core) * half

    def aligned(start):
        return pl.multiple_of(start, TILE)

    tables = [
        pltpu.make_async_copy(rows_hbm, rows_ref, load_sem.at[3 + model]),
        pltpu.make_async_copy(cols_hbm, cols_ref, load_sem.at[4 + model]),
    ]
    loads = [
        pltpu.make_async_copy(up_hbm, up, load_sem.at[0]),
        *(
            pltpu.make_async_copy(tok_hbm.at[:, b * block : (b + 1) * block], tok.at[b], load_sem.at[3 + b])
            for b in range(model)
        ),
        pltpu.make_async_copy(down_hbm, down, load_sem.at[1]),
        pltpu.make_async_copy(target_hbm.at[pl.ds(aligned(mine), half)], target, load_sem.at[2]),
    ]
    barrier = pltpu.get_barrier_semaphore()
    for device in (partner, across, twin):
        pl.semaphore_signal(barrier, inc=1, device_id=device, device_id_type=MESH)
    for load in tables + loads:
        load.start()
    pl.semaphore_wait(barrier, 3)

    def remote(src, dst, sems, where, device):
        return pltpu.make_async_remote_copy(
            src_ref=src, dst_ref=dst, send_sem=sems.at[(0, *where)], recv_sem=sems.at[(1, *where)],
            device_id=device, device_id_type=MESH,
        )

    def weights_to_partner(which, p):
        span = pl.ds(p * PIECE, PIECE)
        return remote((up_hbm, down_hbm)[which].at[span], peer.at[which, span], weight_sem, (which, p), partner)

    everything = [(which, p) for which in range(2) for p in range(pieces)]

    def send_pieces(first, last):
        for which, p in everything[first:last]:
            weights_to_partner(which, p).start()

    cut = [sum(EARLY[: i + 1]) for i in range(3)]
    send_pieces(0, cut[0])

    for table in tables:
        table.wait()
    rank_blocks(cols_ref, rank)
    in_order(rank, lambda k: k, col_block)
    in_order(rank, lambda k: rows_ref[k], col_row)
    rank_blocks(rows_ref, rank)
    in_order(rank, lambda k: k, row_block)
    in_order(rank, lambda k: cols_ref[k], row_col)
    in_order(rank, lambda k: rows_ref[k], row_row)
    keep[0] = 0

    @pl.loop(1, blocks)
    def _(j):
        keep[j] = equal(row_row[j], row_row[j - 1])

    @pl.loop(0, model)
    def _(b):
        upto, here = jnp.int32(0), jnp.int32(0)
        for k in range(blocks):
            upto += less(rows_ref[k], b + 1)
            here += equal(rows_ref[k], b)
        slot[b] = upto * jnp.minimum(here, 1)

    seg[0] = jnp.zeros_like(seg[0])
    for load in loads[:-1]:
        load.wait()

    def sum_by_row(left, right, contract, span):
        @pl.loop(0, blocks)
        def _(j):
            product = dot(left[row_col[j], span, :], right[row_block[j]], contract)
            seg[j + 1] = product + seg[j] * keep[j].astype(F32)

    def forward(base):
        span = pl.ds(aligned(base), TILE)

        @pl.loop(0, hidden)
        def _(h):
            first, second = (
                dot(tok[col_row[2 * h + i], span, :], up[col_block[2 * h + i]], NN) for i in range(2)
            )
            v = (first + second) * scale_in
            pre[h, span, :] = v
            act[h, span, :] = (v * sigmoid(v)).astype(BF16)

        sum_by_row(act, down, NN, span)
        for b in range(model):
            part[span, b * block : (b + 1) * block] = (seg[slot[b]] * scale_out).astype(BF16)

    def backward(base, err, i):
        span, near = pl.ds(aligned(base + i * TILE), TILE), pl.ds(aligned(i * TILE), TILE)

        @pl.loop(0, hidden)
        def _(h):
            first, second = (
                dot(err[col_row[2 * h + n], near, :], down[col_block[2 * h + n]], NT) for n in range(2)
            )
            dact = (first + second) * scale_out
            v = pre[h, span, :]
            sig = sigmoid(v)
            dpre[h, span, :] = (dact * sig * (1.0 + v * (1.0 - sig))).astype(BF16)

        sum_by_row(dpre, up, NT, span)
        per_owner = gpart.shape[2] // block
        for b in range(model):
            at = (b % per_owner) * block
            gpart[b // per_owner, span, at : at + block] = (seg[slot[b]] * scale_in).astype(BF16)

    def up_half(k):
        return pre.at[k // 2, pl.ds(pl.multiple_of((k % 2) * block, block), block)]

    def rows(base, i):
        return pl.ds(aligned(base + i * TILE), TILE)

    def part_to_twin(i):
        return remote(part.at[rows(other, i)], out_twin.at[rows(0, i)], out_sem, (0, i), twin)

    def sum_to_across(i):
        return remote(out_sum.at[rows(0, i)], out_across.at[rows(0, i)], out_sem, (1, i), across)

    def error_to_twin(i):
        return remote(err_mine.at[:, rows(0, i)], err_other.at[:, rows(0, i)], out_sem, (2, i), twin)

    def grad_to_twin(which, base, i):
        owner = (far, chip)[which]
        q = base // TILE + i
        return remote(
            gpart.at[2 * owner + 1 - core, rows(base, i)], grad_twin.at[which, rows(base, i)], grad_sem, (which, q), twin
        )

    def grad_to_across(base, i):
        q = base // TILE + i
        return remote(grad_sum.at[rows(base, i)], grad_across.at[rows(base, i)], grad_sem, (2, q), across)

    def strips(size, body):
        @pl.loop(0, TILE // size)
        def _(s):
            body(s * size)

    @pl.loop(0, steps)
    def _(i):
        forward(other + i * TILE)
        part_to_twin(i).start()

    @pl.loop(0, steps)
    def _(i):
        forward(mine + i * TILE)
        part_to_twin(i).wait_recv()

        def body(s):
            local = pl.ds(pl.multiple_of(i * TILE + s, 32), 32)
            whole = pl.ds(pl.multiple_of(mine + i * TILE + s, 32), 32)
            out_sum[local, :] = (part[whole, :].astype(F32) + out_twin[local, :].astype(F32)).astype(BF16)

        strips(32, body)
        sum_to_across(i).start()

    send_pieces(cut[0], cut[1])
    loads[-1].wait()

    @pl.loop(0, steps)
    def _(i):
        sum_to_across(i).wait_recv()

        def body(s):
            local = pl.ds(pl.multiple_of(i * TILE + s, 32), 32)
            output = out_sum[local, :].astype(F32) + out_across[local, :].astype(F32)
            error = (output - target[local, :].astype(F32)).astype(BF16)
            for b in range(model):
                err_mine[b, local, :] = error[:, b * block : (b + 1) * block]

        strips(32, body)
        error_to_twin(i).start()
        backward(mine, err_mine, i)
        grad_to_twin(0, mine, i).start()
        grad_to_twin(1, mine, i).start()

    send_pieces(cut[1], cut[2])

    @pl.loop(0, steps)
    def _(i):
        error_to_twin(i).wait_recv()

    def pass_on(base, i):
        grad_to_twin(0, base, i).wait_recv()

        def body(s):
            whole = pl.ds(pl.multiple_of(base + i * TILE + s, 64), 64)
            total = gpart[2 * far + core, whole, :].astype(F32) + grad_twin[0, whole, :].astype(F32)
            grad_sum[whole, :] = total.astype(BF16)

        strips(64, body)
        grad_to_across(base, i).start()

    def finish(base, i):
        grad_to_twin(1, base, i).wait_recv()
        grad_to_across(base, i).wait_recv()

        def body(s):
            whole = pl.ds(pl.multiple_of(base + i * TILE + s, 64), 64)
            total = gpart[2 * chip + core, whole, :].astype(F32) + grad_twin[1, whole, :].astype(F32)
            grad[whole, :] = (total + grad_across[whole, :].astype(F32)).astype(BF16)

        strips(64, body)

    @pl.loop(0, steps)
    def _(i):
        backward(other, err_other, i)
        grad_to_twin(0, other, i).start()
        grad_to_twin(1, other, i).start()
        pass_on(other, i)
        pass_on(mine, i)

    send_pieces(cut[2], len(everything))

    @pl.loop(0, blocks)
    def _(k):
        h = cols_ref[k]
        grad_down = dot(act[h, pl.ds(aligned(mine), half), :], err_mine[rows_ref[k]], TN)
        grad_down += dot(act[h, pl.ds(aligned(other), half), :], err_other[rows_ref[k]], TN)
        down_half[k] = 0.5 * down[k].astype(F32) - (STEP_RATE * scale_out) * grad_down
        grad_up = dot(tok[rows_ref[k]], dpre[h], TN)
        up_half(k)[...] = 0.5 * up[k].astype(F32) - (STEP_RATE * scale_in) * grad_up

    @pl.loop(0, steps)
    def _(i):
        finish(other, i)
        finish(mine, i)

    for which, (held, new) in enumerate(((up_half, new_up), (lambda k: down_half.at[k], new_down))):

        @pl.loop(0, pieces)
        def _(p):
            weights_to_partner(which, p).wait_recv()
            for b in range(PIECE):
                k = p * PIECE + b
                new[k] = (held(k)[...] + 0.5 * peer[which, k].astype(F32)).astype(BF16)

        @pl.loop(0, pieces)
        def _(p):
            weights_to_partner(which, p).wait_send()

    @pl.loop(0, steps)
    def _(i):
        part_to_twin(i).wait_send()
        sum_to_across(i).wait_send()
        error_to_twin(i).wait_send()
        for base in (mine, other):
            grad_to_twin(0, base, i).wait_send()
            grad_to_twin(1, base, i).wait_send()
            grad_to_across(base, i).wait_send()


def store_kernel(*refs):
    sources, targets, sems = refs[:3], refs[3:6], refs[6]
    copies = []
    for i, (source, target) in enumerate(zip(sources, targets)):
        size = source.shape[0] // STORES
        for j in range(STORES):
            span = pl.ds(j * size, size)
            copies.append(pltpu.make_async_copy(source.at[span], target.at[span], sems.at[i, j]))
    for copy in copies:
        copy.start()
    for copy in copies:
        copy.wait()


def on_device(tokens, targets, up_weight, down_weight, block_rows, block_columns):
    tok_count, width = tokens.shape
    up_local, down_local = up_weight[0], down_weight[0]
    blocks, block, _ = up_local.shape
    model = width // block
    tensor_count = lax.axis_size("tensor")
    hidden = H // (tensor_count * block)
    scale_in = (D // 4) ** (-0.5)
    scale_out = (H // 4) ** (-0.5)
    apart = (lax.axis_size("dp").bit_length() - 1) // 2
    half, owned = tok_count // 2, width // tensor_count
    steps, pieces = half // TILE, blocks // PIECE
    vmem, dma = pltpu.VMEM, pltpu.SemaphoreType.DMA
    anywhere = pl.BlockSpec(memory_space=pl.ANY)
    weights = vmem((blocks, block, block), BF16)
    flops = 12 * tok_count * blocks * block * block
    new_up, new_down, input_grad = pl.pallas_call(
        lambda *refs: step_kernel(apart, scale_in, scale_out, *refs),
        out_shape=[weights, weights, vmem((tok_count, owned), BF16)],
        in_specs=[anywhere] * 6,
        out_specs=[pl.BlockSpec(memory_space=vmem)] * 3,
        scratch_shapes=[
            vmem((model, tok_count, block), BF16),
            vmem((half, width), BF16),
            vmem((blocks, block, block), BF16),
            vmem((blocks, block, block), BF16),
            vmem((hidden, tok_count, block), F32),
            vmem((hidden, tok_count, block), BF16),
            vmem((hidden, tok_count, block), BF16),
            vmem((blocks + 1, TILE, block), F32),
            vmem((tok_count, width), BF16),
            vmem((model, half, block), BF16),
            vmem((model, half, block), BF16),
            vmem((tensor_count, tok_count, owned), BF16),
            vmem((half, width), BF16),
            vmem((half, width), BF16),
            vmem((half, width), BF16),
            vmem((2, tok_count, owned), BF16),
            vmem((tok_count, owned), BF16),
            vmem((tok_count, owned), BF16),
            vmem((2, blocks, block, block), BF16),
            vmem((blocks, block, block), F32),
            *[pltpu.SMEM((blocks,), jnp.int32)] * 9,
            pltpu.SMEM((model,), jnp.int32),
            dma((5 + model,)),
            dma((2, 2, pieces)),
            dma((2, 3, steps)),
            dma((2, 3, 2 * steps)),
        ],
        compiler_params=pltpu.CompilerParams(
            collective_id=0, has_side_effects=True, vmem_limit_bytes=VMEM_LIMIT
        ),
        cost_estimate=pl.CostEstimate(flops=flops, bytes_accessed=20 << 20, transcendentals=0),
    )(block_rows, block_columns, tokens, targets, up_local, down_local)
    new_up, new_down, input_grad = pl.pallas_call(
        store_kernel,
        out_shape=[jax.ShapeDtypeStruct(a.shape, a.dtype) for a in (new_up, new_down, input_grad)],
        in_specs=[pl.BlockSpec(memory_space=vmem)] * 3,
        out_specs=[anywhere] * 3,
        scratch_shapes=[dma((3, STORES))],
        compiler_params=pltpu.CompilerParams(vmem_limit_bytes=1 << 20),
        cost_estimate=pl.CostEstimate(flops=0, bytes_accessed=10 << 20, transcendentals=0),
    )(new_up, new_down, input_grad)
    return (new_up[None], new_down[None], input_grad)


def solution(mesh):
    return jax.shard_map(
        on_device,
        mesh=mesh,
        in_specs=(
            P("dp", None),
            P("dp", None),
            P("dp", "tensor", None, None),
            P("dp", "tensor", None, None),
            P("tensor"),
            P("tensor"),
        ),
        out_specs=(P("dp", "tensor", None, None), P("dp", "tensor", None, None), P("dp", "tensor")),
        check_vma=False,
    )
```

```python
import jax
import jax.numpy as jnp
from jax import lax
from jax.experimental import pallas as pl
from jax.experimental.pallas import tpu as pltpu
from jax.sharding import PartitionSpec as P

D = 2048
H = 8192
STEP_RATE = 0.5
MESH = pl.DeviceIdType.MESH
F32 = jnp.float32
BF16 = jnp.bfloat16
TILE = 128
PIECE = 2
VMEM_LIMIT = 54 << 20
STORES = 4
EARLY = (5, 6, 2)


def dot(a, b, contract):
    return lax.dot_general(a, b, (contract, ((), ())), preferred_element_type=F32)


NN = ((1,), (0,))
NT = ((1,), (1,))
TN = ((0,), (0,))


def sigmoid(v):
    return 1.0 / (1.0 + jnp.exp(-v))


def equal(a, b):
    return 1 - jnp.minimum((a - b) * (a - b), 1)


def less(a, b):
    return jnp.clip(b - a, 0, 1)


def rank_blocks(values_ref, rank_ref):
    n = values_ref.shape[0]

    @pl.loop(0, n)
    def _(k):
        own = values_ref[k] * n + k
        rank = jnp.int32(0)
        for j in range(n):
            rank += less(values_ref[j] * n + j, own)
        rank_ref[k] = rank


def in_order(rank_ref, value, place_ref):
    n = rank_ref.shape[0]

    @pl.loop(0, n)
    def _(i):
        place = jnp.int32(0)
        for k in range(n):
            place += value(k) * equal(rank_ref[k], i)
        place_ref[i] = place


def step_kernel(
    apart, scale_in, scale_out,
    rows_hbm, cols_hbm, tok_hbm, target_hbm, up_hbm, down_hbm,
    new_up, new_down, grad,
    tok, target, up, down, pre, act, dpre, seg, part, err_mine, err_other, gpart,
    out_twin, out_sum, out_across, grad_twin, grad_sum, grad_across,
    peer, down_half,
    rows_ref, cols_ref, rank, col_block, col_row, row_block, row_col, row_row, keep, slot,
    load_sem, weight_sem, out_sem, grad_sem,
):
    hidden, tok_count, block = pre.shape
    blocks = up.shape[0]
    model = tok.shape[0]
    half = tok_count // 2
    steps = half // TILE
    pieces = blocks // PIECE

    dp, t = lax.axis_index("dp"), lax.axis_index("tensor")
    twin, across, partner = (dp, t ^ 1), (dp, t ^ 2), (dp ^ (1 << apart), t)
    chip, core = t // 2, t % 2
    far = 1 - chip
    mine, other = core * half, (1 - core) * half

    def aligned(start):
        return pl.multiple_of(start, TILE)

    tables = [
        pltpu.make_async_copy(rows_hbm, rows_ref, load_sem.at[3 + model]),
        pltpu.make_async_copy(cols_hbm, cols_ref, load_sem.at[4 + model]),
    ]
    loads = [
        pltpu.make_async_copy(up_hbm, up, load_sem.at[0]),
        *(
            pltpu.make_async_copy(tok_hbm.at[:, b * block : (b + 1) * block], tok.at[b], load_sem.at[3 + b])
            for b in range(model)
        ),
        pltpu.make_async_copy(down_hbm, down, load_sem.at[1]),
        pltpu.make_async_copy(target_hbm.at[pl.ds(aligned(mine), half)], target, load_sem.at[2]),
    ]
    barrier = pltpu.get_barrier_semaphore()
    for device in (partner, across, twin):
        pl.semaphore_signal(barrier, inc=1, device_id=device, device_id_type=MESH)
    for load in tables + loads:
        load.start()
    pl.semaphore_wait(barrier, 3)

    def remote(src, dst, sems, where, device):
        return pltpu.make_async_remote_copy(
            src_ref=src, dst_ref=dst, send_sem=sems.at[(0, *where)], recv_sem=sems.at[(1, *where)],
            device_id=device, device_id_type=MESH,
        )

    def weights_to_partner(which, p):
        span = pl.ds(p * PIECE, PIECE)
        return remote((up_hbm, down_hbm)[which].at[span], peer.at[which, span], weight_sem, (which, p), partner)

    everything = [(which, p) for which in range(2) for p in range(pieces)]

    def send_pieces(first, last):
        for which, p in everything[first:last]:
            weights_to_partner(which, p).start()

    cut = [sum(EARLY[: i + 1]) for i in range(3)]
    send_pieces(0, cut[0])

    for table in tables:
        table.wait()
    rank_blocks(cols_ref, rank)
    in_order(rank, lambda k: k, col_block)
    in_order(rank, lambda k: rows_ref[k], col_row)
    rank_blocks(rows_ref, rank)
    in_order(rank, lambda k: k, row_block)
    in_order(rank, lambda k: cols_ref[k], row_col)
    in_order(rank, lambda k: rows_ref[k], row_row)
    keep[0] = 0

    @pl.loop(1, blocks)
    def _(j):
        keep[j] = equal(row_row[j], row_row[j - 1])

    @pl.loop(0, model)
    def _(b):
        upto, here = jnp.int32(0), jnp.int32(0)
        for k in range(blocks):
            upto += less(rows_ref[k], b + 1)
            here += equal(rows_ref[k], b)
        slot[b] = upto * jnp.minimum(here, 1)

    seg[0] = jnp.zeros_like(seg[0])
    for load in loads[:-1]:
        load.wait()

    def sum_by_row(left, right, contract, span):
        @pl.loop(0, blocks)
        def _(j):
            product = dot(left[row_col[j], span, :], right[row_block[j]], contract)
            seg[j + 1] = product + seg[j] * keep[j].astype(F32)

    def forward(base):
        span = pl.ds(aligned(base), TILE)

        @pl.loop(0, hidden)
        def _(h):
            first, second = (
                dot(tok[col_row[2 * h + i], span, :], up[col_block[2 * h + i]], NN) for i in range(2)
            )
            v = (first + second) * scale_in
            pre[h, span, :] = v
            act[h, span, :] = (v * sigmoid(v)).astype(BF16)

        sum_by_row(act, down, NN, span)
        for b in range(model):
            part[span, b * block : (b + 1) * block] = (seg[slot[b]] * scale_out).astype(BF16)

    def backward(base, err, i):
        span, near = pl.ds(aligned(base + i * TILE), TILE), pl.ds(aligned(i * TILE), TILE)

        @pl.loop(0, hidden)
        def _(h):
            first, second = (
                dot(err[col_row[2 * h + n], near, :], down[col_block[2 * h + n]], NT) for n in range(2)
            )
            dact = (first + second) * scale_out
            v = pre[h, span, :]
            sig = sigmoid(v)
            dpre[h, span, :] = (dact * sig * (1.0 + v * (1.0 - sig))).astype(BF16)

        sum_by_row(dpre, up, NT, span)
        per_owner = gpart.shape[2] // block
        for b in range(model):
            at = (b % per_owner) * block
            gpart[b // per_owner, span, at : at + block] = (seg[slot[b]] * scale_in).astype(BF16)

    def up_half(k):
        return pre.at[k // 2, pl.ds(pl.multiple_of((k % 2) * block, block), block)]

    def rows(base, i):
        return pl.ds(aligned(base + i * TILE), TILE)

    def part_to_twin(i):
        return remote(part.at[rows(other, i)], out_twin.at[rows(0, i)], out_sem, (0, i), twin)

    def sum_to_across(i):
        return remote(out_sum.at[rows(0, i)], out_across.at[rows(0, i)], out_sem, (1, i), across)

    def error_to_twin(i):
        return remote(err_mine.at[:, rows(0, i)], err_other.at[:, rows(0, i)], out_sem, (2, i), twin)

    def grad_to_twin(which, base, i):
        owner = (far, chip)[which]
        q = base // TILE + i
        return remote(
            gpart.at[2 * owner + 1 - core, rows(base, i)], grad_twin.at[which, rows(base, i)], grad_sem, (which, q), twin
        )

    def grad_to_across(base, i):
        q = base // TILE + i
        return remote(grad_sum.at[rows(base, i)], grad_across.at[rows(base, i)], grad_sem, (2, q), across)

    def strips(size, body):
        @pl.loop(0, TILE // size)
        def _(s):
            body(s * size)

    @pl.loop(0, steps)
    def _(i):
        forward(other + i * TILE)
        part_to_twin(i).start()

    @pl.loop(0, steps)
    def _(i):
        forward(mine + i * TILE)
        part_to_twin(i).wait_recv()

        def body(s):
            local = pl.ds(pl.multiple_of(i * TILE + s, 32), 32)
            whole = pl.ds(pl.multiple_of(mine + i * TILE + s, 32), 32)
            out_sum[local, :] = (part[whole, :].astype(F32) + out_twin[local, :].astype(F32)).astype(BF16)

        strips(32, body)
        sum_to_across(i).start()

    send_pieces(cut[0], cut[1])
    loads[-1].wait()

    @pl.loop(0, steps)
    def _(i):
        sum_to_across(i).wait_recv()

        def body(s):
            local = pl.ds(pl.multiple_of(i * TILE + s, 32), 32)
            output = out_sum[local, :].astype(F32) + out_across[local, :].astype(F32)
            error = (output - target[local, :].astype(F32)).astype(BF16)
            for b in range(model):
                err_mine[b, local, :] = error[:, b * block : (b + 1) * block]

        strips(32, body)
        error_to_twin(i).start()
        backward(mine, err_mine, i)
        grad_to_twin(0, mine, i).start()
        grad_to_twin(1, mine, i).start()

    send_pieces(cut[1], cut[2])

    @pl.loop(0, steps)
    def _(i):
        error_to_twin(i).wait_recv()

    def pass_on(base, i):
        grad_to_twin(0, base, i).wait_recv()

        def body(s):
            whole = pl.ds(pl.multiple_of(base + i * TILE + s, 64), 64)
            total = gpart[2 * far + core, whole, :].astype(F32) + grad_twin[0, whole, :].astype(F32)
            grad_sum[whole, :] = total.astype(BF16)

        strips(64, body)
        grad_to_across(base, i).start()

    def finish(base, i):
        grad_to_twin(1, base, i).wait_recv()
        grad_to_across(base, i).wait_recv()

        def body(s):
            whole = pl.ds(pl.multiple_of(base + i * TILE + s, 64), 64)
            total = gpart[2 * chip + core, whole, :].astype(F32) + grad_twin[1, whole, :].astype(F32)
            grad[whole, :] = (total + grad_across[whole, :].astype(F32)).astype(BF16)

        strips(64, body)

    @pl.loop(0, steps)
    def _(i):
        backward(other, err_other, i)
        grad_to_twin(0, other, i).start()
        grad_to_twin(1, other, i).start()
        pass_on(other, i)
        pass_on(mine, i)

    send_pieces(cut[2], len(everything))

    @pl.loop(0, blocks)
    def _(k):
        h = cols_ref[k]
        grad_down = dot(act[h, pl.ds(aligned(mine), half), :], err_mine[rows_ref[k]], TN)
        grad_down += dot(act[h, pl.ds(aligned(other), half), :], err_other[rows_ref[k]], TN)
        down_half[k] = 0.5 * down[k].astype(F32) - (STEP_RATE * scale_out) * grad_down
        grad_up = dot(tok[rows_ref[k]], dpre[h], TN)
        up_half(k)[...] = 0.5 * up[k].astype(F32) - (STEP_RATE * scale_in) * grad_up

    @pl.loop(0, steps)
    def _(i):
        finish(other, i)
        finish(mine, i)

    for which, (held, new) in enumerate(((up_half, new_up), (lambda k: down_half.at[k], new_down))):

        @pl.loop(0, pieces)
        def _(p):
            weights_to_partner(which, p).wait_recv()
            for b in range(PIECE):
                k = p * PIECE + b
                new[k] = (held(k)[...] + 0.5 * peer[which, k].astype(F32)).astype(BF16)

        @pl.loop(0, pieces)
        def _(p):
            weights_to_partner(which, p).wait_send()

    @pl.loop(0, steps)
    def _(i):
        part_to_twin(i).wait_send()
        sum_to_across(i).wait_send()
        error_to_twin(i).wait_send()
        for base in (mine, other):
            grad_to_twin(0, base, i).wait_send()
            grad_to_twin(1, base, i).wait_send()
            grad_to_across(base, i).wait_send()


def store_kernel(*refs):
    sources, targets, sems = refs[:3], refs[3:6], refs[6]
    copies = []
    for i, (source, target) in enumerate(zip(sources, targets)):
        size = source.shape[0] // STORES
        for j in range(STORES):
            span = pl.ds(j * size, size)
            copies.append(pltpu.make_async_copy(source.at[span], target.at[span], sems.at[i, j]))
    for copy in copies:
        copy.start()
    for copy in copies:
        copy.wait()


def on_device(tokens, targets, up_weight, down_weight, block_rows, block_columns):
    tok_count, width = tokens.shape
    up_local, down_local = up_weight[0], down_weight[0]
    blocks, block, _ = up_local.shape
    model = width // block
    tensor_count = lax.axis_size("tensor")
    hidden = H // (tensor_count * block)
    scale_in = (D // 4) ** (-0.5)
    scale_out = (H // 4) ** (-0.5)
    apart = (lax.axis_size("dp").bit_length() - 1) // 2
    half, owned = tok_count // 2, width // tensor_count
    steps, pieces = half // TILE, blocks // PIECE
    vmem, dma = pltpu.VMEM, pltpu.SemaphoreType.DMA
    anywhere = pl.BlockSpec(memory_space=pl.ANY)
    weights = vmem((blocks, block, block), BF16)
    flops = 12 * tok_count * blocks * block * block
    new_up, new_down, input_grad = pl.pallas_call(
        lambda *refs: step_kernel(apart, scale_in, scale_out, *refs),
        out_shape=[weights, weights, vmem((tok_count, owned), BF16)],
        in_specs=[anywhere] * 6,
        out_specs=[pl.BlockSpec(memory_space=vmem)] * 3,
        scratch_shapes=[
            vmem((model, tok_count, block), BF16),
            vmem((half, width), BF16),
            vmem((blocks, block, block), BF16),
            vmem((blocks, block, block), BF16),
            vmem((hidden, tok_count, block), F32),
            vmem((hidden, tok_count, block), BF16),
            vmem((hidden, tok_count, block), BF16),
            vmem((blocks + 1, TILE, block), F32),
            vmem((tok_count, width), BF16),
            vmem((model, half, block), BF16),
            vmem((model, half, block), BF16),
            vmem((tensor_count, tok_count, owned), BF16),
            vmem((half, width), BF16),
            vmem((half, width), BF16),
            vmem((half, width), BF16),
            vmem((2, tok_count, owned), BF16),
            vmem((tok_count, owned), BF16),
            vmem((tok_count, owned), BF16),
            vmem((2, blocks, block, block), BF16),
            vmem((blocks, block, block), F32),
            *[pltpu.SMEM((blocks,), jnp.int32)] * 9,
            pltpu.SMEM((model,), jnp.int32),
            dma((5 + model,)),
            dma((2, 2, pieces)),
            dma((2, 3, steps)),
            dma((2, 3, 2 * steps)),
        ],
        compiler_params=pltpu.CompilerParams(
            collective_id=0, has_side_effects=True, vmem_limit_bytes=VMEM_LIMIT
        ),
        cost_estimate=pl.CostEstimate(flops=flops, bytes_accessed=20 << 20, transcendentals=0),
    )(block_rows, block_columns, tokens, targets, up_local, down_local)
    new_up, new_down, input_grad = pl.pallas_call(
        store_kernel,
        out_shape=[jax.ShapeDtypeStruct(a.shape, a.dtype) for a in (new_up, new_down, input_grad)],
        in_specs=[pl.BlockSpec(memory_space=vmem)] * 3,
        out_specs=[anywhere] * 3,
        scratch_shapes=[dma((3, STORES))],
        compiler_params=pltpu.CompilerParams(vmem_limit_bytes=1 << 20),
        cost_estimate=pl.CostEstimate(flops=0, bytes_accessed=10 << 20, transcendentals=0),
    )(new_up, new_down, input_grad)
    return (new_up[None], new_down[None], input_grad)


def solution(mesh):
    return jax.shard_map(
        on_device,
        mesh=mesh,
        in_specs=(
            P("dp", None),
            P("dp", None),
            P("dp", "tensor", None, None),
            P("dp", "tensor", None, None),
            P("tensor"),
            P("tensor"),
        ),
        out_specs=(P("dp", "tensor", None, None), P("dp", "tensor", None, None), P("dp", "tensor")),
        check_vma=False,
    )
```
